128 devices in a mesh: row: 16 (over z_hi, y, core), col: 8 (over x, z_lo).
Axes of the slice: x: 4, y: 4, z: 4 (z_hi: 2, z_lo: 2; z = z_hi * 2 + z_lo), core: 2. Of those that a mesh axis runs over, the one named last changes fastest.
Arguments:
- context: bfloat16 [256, 512, 384], P('row', 'col'), may hold values from -6 to 6
- first_dilated_weight: bfloat16 [3, 3, 384, 384], replicated, may hold values from -0.109375 to 0.109375
- first_plain_weight: bfloat16 [3, 3, 384, 384], replicated, may hold values from -0.109375 to 0.109375
- second_dilated_weight: bfloat16 [3, 3, 384, 384], replicated, may hold values from -0.109375 to 0.109375
- second_plain_weight: bfloat16 [3, 3, 384, 384], replicated, may hold values from -0.109375 to 0.109375
- lift_weight: bfloat16 [384, 1536], replicated, may hold values from -0.3125 to 0.3125
- fine_weight: bfloat16 [3, 3, 96, 96], replicated, may hold values from -0.21875 to 0.21875
Outputs:
- context_out: bfloat16 [256, 512, 384], P('row', 'col')
- target: bfloat16 [256, 512, 96], P('row', 'col')
The draws below stay inside these ranges and needn't reach their ends.
All inputs are finite; a program needn't handle non-finite values.
Results may differ from the reference program's by a relative error of at most 0.015.
Values may be sent and summed in bfloat16 or wider, within the bound.
No kernel may reach another device: no remote copies, remote signals or barrier semaphores. Data moves between devices by JAX's collectives and lax.ppermute only.
A program may use at most 64 MiB of HBM per device.

```python
import jax
import jax.numpy as jnp
from jax import lax

C = 384
F = 96
FIRST_DILATION = 32
SECOND_DILATION = 64
ROWS = 256
COLS = 512
CROP_R = 64
CROP_C = 128


def shard_levels(rng, dims, split, least, top_value):
    loudness, own = 1.0, jax.random.fold_in(rng, 6)
    for position, blocks in split:
        draws = jnp.exp(jax.random.uniform(jax.random.fold_in(own, position), (blocks,), jnp.float32, least / len(split), top_value / len(split)))
        loudness = loudness * jnp.repeat(draws, dims[position] // blocks).reshape([-1 if axis == position else 1 for axis in range(len(dims))])
    return loudness


def centred(rng, dims, deviation, limit, shards=(), kind=jnp.bfloat16):
    values = deviation * jax.random.normal(rng, dims, jnp.float32)
    if shards:
        values = values * shard_levels(rng, dims, shards, -0.22, 0.18)
    return jnp.clip(values, -limit, limit).astype(kind)


def setup_inputs(seed: int = 0) -> dict:
    key_of = jax.random.split(jax.random.key(seed), 8)
    return {
        "context": centred(key_of[0], (ROWS, COLS, C), 1.0, 6.0, ((0, 16), (1, 8))),
        "first_dilated_weight": centred(key_of[1], (3, 3, C, C), (9 * C) ** -0.5, 0.109375),
        "first_plain_weight": centred(key_of[2], (3, 3, C, C), (9 * C) ** -0.5, 0.109375),
        "second_dilated_weight": centred(key_of[3], (3, 3, C, C), (9 * C) ** -0.5, 0.109375),
        "second_plain_weight": centred(key_of[4], (3, 3, C, C), (9 * C) ** -0.5, 0.109375),
        "lift_weight": centred(key_of[5], (C, 16 * F), C ** -0.5, 0.3125),
        "fine_weight": centred(key_of[6], (3, 3, F, F), (9 * F) ** -0.5, 0.21875),
    }


def apply_convolution(field, kernel, tap_spacing):
    result = lax.conv_general_dilated(field[None], kernel, (1, 1), ((tap_spacing, tap_spacing), (tap_spacing, tap_spacing)), rhs_dilation=(tap_spacing, tap_spacing), dimension_numbers=("NHWC", "HWIO", "NHWC"), preferred_element_type=jnp.float32)
    return result[0]


def reference(context, first_dilated_weight, first_plain_weight, second_dilated_weight, second_plain_weight, lift_weight, fine_weight):
    running_state = context
    for dilated_kernel, kernel_border, tap_spacing in ((first_dilated_weight, first_plain_weight, FIRST_DILATION), (second_dilated_weight, second_plain_weight, SECOND_DILATION)):
        hidden_state = jax.nn.silu(apply_convolution(running_state, dilated_kernel, tap_spacing)).astype(jnp.bfloat16)
        running_state = (running_state.astype(jnp.float32) + apply_convolution(hidden_state, kernel_border, 1)).astype(jnp.bfloat16)
    row_start = ROWS // 2
    col_start = COLS // 2
    crop_cells = running_state[row_start:row_start + CROP_R, col_start:col_start + CROP_C]
    lifted = jnp.dot(crop_cells.reshape(CROP_R * CROP_C, C), lift_weight, preferred_element_type=jnp.float32).astype(jnp.bfloat16)
    lifted = lifted.reshape(CROP_R, CROP_C, 4, 4, F).transpose(0, 2, 1, 3, 4).reshape(4 * CROP_R, 4 * CROP_C, F)
    target = apply_convolution(lifted, fine_weight, 1).astype(jnp.bfloat16)
    return running_state, target
```

```python
import jax
import jax.numpy as jnp
from jax import lax
from jax.sharding import Mesh, PartitionSpec as P

AXES = ("zh", "y1", "y0", "core", "x1", "x0", "zl")
ROW = ("zh", "y1", "y0", "core")
COL = ("x1", "x0", "zl")
SPREAD = ("zh", "y1", "y0", "x1", "x0", "zl")
BF16 = jnp.bfloat16
F32 = jnp.float32


def device_of_band(band):
    core, rest = divmod(band, 8)
    return rest * 2 + core


def band_route(step):
    return [(device_of_band(b), device_of_band((b + step) % 16)) for b in range(16)]


def ring_route(step):
    return [(i, (i + step) % 8) for i in range(8)]


def line_route(count, step):
    return [(i, i + step) for i in range(count) if 0 <= i + step < count]


def dilated(cells, kernel, spacing):
    return lax.conv_general_dilated(
        cells, kernel, (1, 1), ((spacing, spacing), (spacing, spacing)),
        rhs_dilation=(spacing, spacing), dimension_numbers=("HWNC", "HWIO", "HWNC"),
        preferred_element_type=F32,
    )


def plain(hidden, state, kernel, first_band, last_band, first_ring, last_ring):
    channels = hidden.shape[-1]
    tiles = hidden.reshape(8, 16, 2, 4, channels)
    up = lax.ppermute(tiles[:, :, 1], ROW, band_route(1))
    down = lax.ppermute(tiles[:, :, 0], ROW, band_route(-1))
    nothing = jnp.zeros((1, 16, 4, channels), BF16)
    up = jnp.where(first_band, jnp.concatenate([nothing, up[:-1]], 0), up)
    down = jnp.where(last_band, jnp.concatenate([down[1:], nothing], 0), down)
    above = jnp.concatenate([up[:, :, None], tiles[:, :, :1]], 2)
    below = jnp.concatenate([tiles[:, :, 1:], down[:, :, None]], 2)
    stack = jnp.concatenate([t.reshape(1024, channels) for t in (above, tiles, below)], 1)
    weights = [kernel[:, b].reshape(3 * channels, channels) for b in range(3)]
    to_right, centre, to_left = (
        jnp.dot(stack, w, preferred_element_type=F32).reshape(8, 16, 2, 4, channels)
        for w in weights
    )
    from_left = lax.ppermute(to_right[:, :, :, 3].astype(BF16), COL, ring_route(1))
    from_right = lax.ppermute(to_left[:, :, :, 0].astype(BF16), COL, ring_route(-1))
    nothing = jnp.zeros((8, 1, 2, channels), BF16)
    from_left = jnp.where(first_ring, jnp.concatenate([nothing, from_left[:, :-1]], 1), from_left)
    from_right = jnp.where(last_ring, jnp.concatenate([from_right[:, 1:], nothing], 1), from_right)
    total = (
        centre
        + jnp.concatenate([from_left[:, :, :, None].astype(F32), to_right[:, :, :, :3]], 3)
        + jnp.concatenate([to_left[:, :, :, 1:], from_right[:, :, :, None].astype(F32)], 3)
    )
    return (state.astype(F32) + total.reshape(8, 16, 8, channels)).astype(BF16)


def crop_route():
    route = []
    for bits in range(128):
        i3, i2, i5, i4, j4, j6, j5 = ((bits >> k) & 1 for k in range(6, -1, -1))
        target = 0
        for bit in (i5, i4, i3, i2, j6, j5, j4):
            target = target * 2 + bit
        route.append((bits, target))
    return route


def fine_target(state, lift_weight, fine_weight):
    channels = state.shape[-1]
    width = fine_weight.shape[-1]
    crop = state[4:6, 8:12].reshape(8, 8, channels)
    crop = lax.all_to_all(crop, ("y0", "x0", "zl"), 0, 0, tiled=True)
    crop = crop.reshape(2, 4, 2, 4, channels).transpose(0, 2, 1, 3, 4).reshape(4, 16, channels)
    crop = lax.ppermute(crop, AXES, crop_route())
    for axis, dim, count in ((ROW, 0, 16), (COL, 1, 8)):
        size = crop.shape[dim]
        low = lax.ppermute(lax.slice_in_dim(crop, size - 1, size, axis=dim), axis, line_route(count, 1))
        high = lax.ppermute(lax.slice_in_dim(crop, 0, 1, axis=dim), axis, line_route(count, -1))
        crop = jnp.concatenate([low, crop, high], dim)
    lifted = jnp.einsum("rcf,fg->rcg", crop, lift_weight, preferred_element_type=F32).astype(BF16)
    lifted = lifted.reshape(6, 18, 4, 4, width).transpose(0, 2, 1, 3, 4).reshape(24, 72, width)
    lifted = lifted[3:21, 3:69]
    target = lax.conv_general_dilated(
        lifted[None], fine_weight, (1, 1), ((0, 0), (0, 0)),
        dimension_numbers=("NHWC", "HWIO", "NHWC"), preferred_element_type=F32,
    )
    return target[0].astype(BF16)


def shards(context, first_dilated_weight, first_plain_weight, second_dilated_weight,
           second_plain_weight, lift_weight, fine_weight):
    channels = context.shape[-1]
    band = 8 * lax.axis_index("core") + lax.axis_index(("zh", "y1", "y0"))
    ring = lax.axis_index(COL)
    ends = (band == 0, band == 15, ring == 0, ring == 7)
    sent = context.reshape(8, 2, 2, 8, 4, channels).transpose(0, 3, 2, 1, 4, 5)
    state = lax.all_to_all(sent.reshape(64, 16, channels), SPREAD, 0, 0, tiled=True)
    state = state.reshape(8, 16, 8, channels)
    for dilated_kernel, plain_kernel, spacing in (
        (first_dilated_weight, first_plain_weight, 1),
        (second_dilated_weight, second_plain_weight, 2),
    ):
        hidden = jax.nn.silu(dilated(state, dilated_kernel, spacing)).astype(BF16)
        state = plain(hidden, state, plain_kernel, *ends)
    target = fine_target(state, lift_weight, fine_weight)
    back = lax.all_to_all(state.reshape(64, 16, channels), SPREAD, 0, 0, tiled=True)
    back = back.reshape(8, 8, 2, 2, 4, channels).transpose(0, 3, 2, 1, 4, 5)
    return back.reshape(16, 64, channels), target


def solution(mesh):
    fine_mesh = Mesh(mesh.devices.reshape((2,) * 7), AXES)
    return jax.shard_map(
        shards,
        mesh=fine_mesh,
        in_specs=(P(ROW, COL, None), P(), P(), P(), P(), P(), P()),
        out_specs=(P(ROW, COL, None), P(ROW, COL, None)),
        check_vma=False,
    )
```

```python
import jax
import jax.numpy as jnp
from jax import lax
from jax.experimental import pallas as pl
from jax.experimental.pallas import tpu as pltpu
from jax.sharding import Mesh, PartitionSpec as P


AXES = ("zh", "y1", "y0", "core", "x1", "x0", "zl")
ROW = ("zh", "y1", "y0", "core")
COL = ("x1", "x0", "zl")
SPREAD = ("zh", "y1", "y0", "x1", "x0", "zl")
BF16 = jnp.bfloat16
F32 = jnp.float32
VMEM = pl.BlockSpec(memory_space=pltpu.VMEM)
SMEM = pl.BlockSpec(memory_space=pltpu.SMEM)


def kernel_call(body, outs, scratch=(), inputs=0, scalars=0, limit=24):
    call = pl.pallas_call(
        body,
        out_shape=[pltpu.VMEM(s, t) for s, t in outs],
        in_specs=[SMEM] * scalars + [VMEM] * inputs,
        out_specs=[VMEM] * len(outs),
        scratch_shapes=[pltpu.VMEM(s, t) for s, t in scratch],
        compiler_params=pltpu.CompilerParams(vmem_limit_bytes=limit << 20),
    )

    def run(*operands):
        near = [pltpu.with_memory_space_constraint(x, pltpu.VMEM) for x in operands[scalars:]]
        return call(*operands[:scalars], *near)

    return run


def device_of_band(band):
    core, rest = divmod(band, 8)
    return rest * 2 + core


def band_route(step):
    return [(device_of_band(b), device_of_band((b + step) % 16)) for b in range(16)]


def ring_route(step):
    return [(i, (i + step) % 8) for i in range(8)]


def line_route(count, step):
    return [(i, i + step) for i in range(count) if 0 <= i + step < count]


def gather_body(context, sent):
    channels = context.shape[-1]
    first = lax.broadcasted_iota(jnp.int32, (4, 8, channels), 1) < 4

    def step(row, carry):
        line = context[row].astype(F32)
        low = line[:32].reshape(4, 8, channels)
        high = line[32:].reshape(4, 8, channels)
        even = jnp.where(first, low, pltpu.roll(high, 4, 1))
        odd = jnp.where(first, pltpu.roll(low, 4, 1), high)
        for pair in range(4):
            place = 8 * (row // 2) + 2 * pair
            sent[place, row % 2] = even[pair].astype(BF16)
            sent[place + 1, row % 2] = odd[pair].astype(BF16)
        return carry

    lax.fori_loop(0, 16, step, 0)


def scatter_body(landed, result):
    channels = result.shape[-1]
    first = lax.broadcasted_iota(jnp.int32, (8, channels), 0) < 4

    def step(row, carry):
        for pair in range(4):
            place = 8 * (row // 2) + 2 * pair
            even = landed[place, row % 2].astype(F32)
            odd = landed[place + 1, row % 2].astype(F32)
            low = jnp.where(first, even, pltpu.roll(odd, 4, 0))
            high = jnp.where(first, pltpu.roll(even, 4, 0), odd)
            result[row, 8 * pair : 8 * pair + 8] = low.astype(BF16)
            result[row, 32 + 8 * pair : 40 + 8 * pair] = high.astype(BF16)
        return carry

    lax.fori_loop(0, 16, step, 0)


def dilated_band(cells, kernel, hidden, shelves, spacing):
    channels = cells.shape[-1]
    reach = 4 * spacing
    place = lax.broadcasted_iota(jnp.int32, cells.shape, 1)
    left = jnp.where(place < reach, 0.0, pltpu.roll(cells, reach, 1))
    right = jnp.where(place >= 64 - reach, 0.0, pltpu.roll(cells, 64 - reach, 1))
    edge = jnp.zeros((spacing, 64, channels), BF16)
    for index, shelf in enumerate((left, cells, right)):
        shelves[index, :spacing] = edge
        shelves[index, spacing : spacing + 8] = shelf.astype(BF16)
        shelves[index, spacing + 8 : spacing + 8 + spacing] = edge
    stack = jnp.concatenate(
        [
            shelves[b, a * spacing : a * spacing + 8].reshape(512, channels)
            for a in range(3)
            for b in range(3)
        ],
        axis=1,
    )
    total = jnp.dot(stack, kernel[...], preferred_element_type=F32)
    hidden[...] = (total / (1.0 + jnp.exp(-total))).astype(BF16)


def first_dilated_body(landed, kernel, hidden0, hidden1, shelves):
    channels = landed.shape[-1]
    for i0, hidden in enumerate((hidden0, hidden1)):
        cells = landed[:, i0].astype(F32).reshape(8, 64, channels)
        dilated_band(cells, kernel, hidden, shelves, 1)


def settle(partial, sums, from_left, from_right, ends, i0, channels):
    place = lax.broadcasted_iota(jnp.int32, (128, channels), 0) % 16
    left = from_left[i0].astype(F32)
    right = from_right[i0].astype(F32)
    left = jnp.where(
        ends[2] == 1, jnp.where(place == 0, 0.0, pltpu.roll(left, 1, 0)), left
    )
    right = jnp.where(
        ends[3] == 1, jnp.where(place == 15, 0.0, pltpu.roll(right, 127, 0)), right
    )
    pieces = []
    for lane in range(0, channels, 128):
        inner = sums.at[i0, lane // 128]
        inner[...] = partial[i0, :, lane : lane + 128]
        inner[pl.ds(0, 128, stride=4)] = inner[pl.ds(0, 128, stride=4)] + left[:, lane : lane + 128]
        inner[pl.ds(3, 128, stride=4)] = inner[pl.ds(3, 128, stride=4)] + right[:, lane : lane + 128]
        pieces.append(inner[...].astype(BF16))
    return jnp.concatenate(pieces, 1)


def second_dilated_body(ends, partial, from_left, from_right, kernel, state, hidden0, hidden1, sums, shelves):
    channels = state.shape[-1]
    for i0, hidden in enumerate((hidden0, hidden1)):
        cells = settle(partial, sums, from_left, from_right, ends, i0, channels)
        state[:, i0] = cells.reshape(64, 8, channels)
        dilated_band(cells.astype(F32).reshape(8, 64, channels), kernel, hidden, shelves, 2)


def final_body(ends, partial, from_left, from_right, state, sums):
    channels = state.shape[-1]
    for i0 in range(2):
        cells = settle(partial, sums, from_left, from_right, ends, i0, channels)
        state[:, i0] = cells.reshape(64, 8, channels)


def edge_body(ends, up, down, hidden0, hidden1, kernel, to_left, to_right, above, below, wide):
    channels = up.shape[-1]
    blank = jnp.zeros((64, channels), BF16)
    above[:64] = blank
    above[64:] = up[...]
    below[:512] = down[...]
    below[512:] = blank
    start = pl.multiple_of(64 - 64 * ends[0], 64)
    lines = [above[pl.ds(start, 512)], hidden0[...], hidden1[...]]
    start = pl.multiple_of(64 * ends[1], 64)
    lines.append(below[pl.ds(start, 512)])
    for index, line in enumerate(lines):
        for lane in range(0, channels, 128):
            wide[index, lane // 128] = line[:, lane : lane + 128].astype(F32)
    for column, tap, sums in ((3, 0, to_right), (0, 2, to_left)):
        weights = kernel[:, tap].reshape(3 * channels, channels)
        lines = [
            jnp.concatenate(
                [
                    wide.at[line, lane][pl.ds(column, 128, stride=4)].astype(BF16)
                    for lane in range(channels // 128)
                ],
                1,
            )
            for line in range(4)
        ]
        stack = jnp.concatenate(
            [jnp.concatenate(lines[:3], 1), jnp.concatenate(lines[1:], 1)], 0
        )
        product = jnp.dot(stack, weights, preferred_element_type=F32).astype(BF16)
        sums[0] = product[:128]
        sums[1] = product[128:]


def plain_body(ends, up, down, hidden0, hidden1, state, kernel, partial, above, below):
    channels = up.shape[-1]
    blank = jnp.zeros((64, channels), BF16)
    above[:64] = blank
    above[64:] = up[...]
    below[:512] = down[...]
    below[512:] = blank
    over = above[pl.ds(pl.multiple_of(64 - 64 * ends[0], 64), 512)]
    under = below[pl.ds(pl.multiple_of(64 * ends[1], 64), 512)]
    lines = (over, hidden0[...], hidden1[...], under)
    place = lax.broadcasted_iota(jnp.int32, (512, channels), 0) % 4
    for i0 in range(2):
        stack = jnp.concatenate(lines[i0 : i0 + 3], 1)
        products = [
            jnp.dot(stack, kernel[:, tap].reshape(3 * channels, channels), preferred_element_type=F32)
            for tap in range(3)
        ]
        total = state[:, i0].reshape(512, channels).astype(F32) + products[1]
        total = total + jnp.where(place == 0, 0.0, pltpu.roll(products[0], 1, 0))
        total = total + jnp.where(place == 3, 0.0, pltpu.roll(products[2], 511, 0))
        partial[i0] = total


def crop_route(shift):
    route = []
    for bits in range(128):
        i3, i2, i5, i4, j4, j6, j5 = ((bits >> k) & 1 for k in range(6, -1, -1))
        row = 8 * i5 + 4 * i4 + 2 * i3 + i2 + shift
        column = 4 * j6 + 2 * j5 + j4
        if 0 <= row < 16:
            route.append((bits, row * 8 + column))
    return route


def crop_cells(state):
    channels = state.shape[-1]
    crop = state.reshape(8, 8, 2, 2, 4, channels)[4:6, 4:6].transpose(0, 1, 3, 2, 4, 5)
    crop = lax.all_to_all(
        crop.reshape(8, 8, channels), ("y0", "x0", "zl"), 0, 0, tiled=True
    )
    crop = crop.reshape(2, 4, 2, 4, channels).transpose(0, 2, 1, 3, 4)
    return crop.reshape(4, 16, channels)


def fine_target(crop, lift_weight, fine_weight):
    width = fine_weight.shape[-1]
    low = lax.ppermute(crop[3:], AXES, crop_route(1))
    high = lax.ppermute(crop[:1], AXES, crop_route(-1))
    crop = lax.ppermute(crop, AXES, crop_route(0))
    crop = jnp.concatenate([low, crop, high], 0)
    low = lax.ppermute(crop[:, 15:], COL, line_route(8, 1))
    high = lax.ppermute(crop[:, :1], COL, line_route(8, -1))
    crop = jnp.concatenate([low, crop, high], 1)
    lifted = jnp.einsum("rcf,fg->rcg", crop, lift_weight, preferred_element_type=F32).astype(BF16)
    lifted = lifted.reshape(6, 18, 4, 4, width).transpose(0, 2, 1, 3, 4).reshape(24, 72, width)
    lifted = lifted[3:21, 3:69]
    target = lax.conv_general_dilated(
        lifted[None], fine_weight, (1, 1), ((0, 0), (0, 0)),
        dimension_numbers=("NHWC", "HWIO", "NHWC"), preferred_element_type=F32,
    )
    return target[0].astype(BF16)


def plain(hidden0, hidden1, state, kernel, ends):
    channels = hidden0.shape[-1]
    up = lax.ppermute(hidden1, ROW, band_route(1))
    down = lax.ppermute(hidden0, ROW, band_route(-1))
    padded = [((576, channels), BF16)] * 2
    to_left, to_right = kernel_call(
        edge_body,
        [((2, 128, channels), BF16)] * 2,
        padded + [((4, 3, 512, 128), F32)],
        5, 1,
    )(ends, up, down, hidden0, hidden1, kernel)
    from_left = lax.ppermute(to_right, COL, ring_route(1))
    from_right = lax.ppermute(to_left, COL, ring_route(-1))
    (partial,) = kernel_call(plain_body, [((2, 512, channels), F32)], padded, 6, 1)(
        ends, up, down, hidden0, hidden1, state, kernel
    )
    return partial, from_left, from_right


def shards(context, first_dilated_weight, first_plain_weight, second_dilated_weight,
           second_plain_weight, lift_weight, fine_weight):
    channels = context.shape[-1]
    band = 8 * lax.axis_index("core") + lax.axis_index(("zh", "y1", "y0"))
    ring = lax.axis_index(COL)
    ends = jnp.array([0, 15, 0, 7]) == jnp.array([1, 1, 0, 0]) * band + jnp.array([0, 0, 1, 1]) * ring
    ends = ends.astype(jnp.int32)
    spread = (64, 2, 8, channels)
    band_shape = ((512, channels), BF16)
    (sent,) = kernel_call(gather_body, [(spread, BF16)], (), 1)(context)
    state = lax.all_to_all(sent, SPREAD, 0, 0, tiled=True)
    hidden0, hidden1 = kernel_call(
        first_dilated_body, [band_shape] * 2, [((3, 10, 64, channels), BF16)], 2
    )(state, first_dilated_weight.reshape(9 * channels, channels))
    edges = plain(hidden0, hidden1, state, first_plain_weight, ends)
    state, hidden0, hidden1 = kernel_call(
        second_dilated_body,
        [(spread, BF16), band_shape, band_shape],
        [((2, 3, 512, 128), F32), ((3, 12, 64, channels), BF16)],
        4, 1,
    )(ends, *edges, second_dilated_weight.reshape(9 * channels, channels))
    edges = plain(hidden0, hidden1, state, second_plain_weight, ends)
    (state,) = kernel_call(
        final_body, [(spread, BF16)], [((2, 3, 512, 128), F32)], 3, 1
    )(ends, *edges)
    crop = crop_cells(state)
    landed = lax.all_to_all(state, SPREAD, 0, 0, tiled=True)
    target = fine_target(crop, lift_weight, fine_weight)
    (result,) = kernel_call(scatter_body, [((16, 64, channels), BF16)], (), 1)(landed)
    return result, target


def solution(mesh):
    fine_mesh = Mesh(mesh.devices.reshape((2,) * 7), AXES)
    return jax.shard_map(
        shards,
        mesh=fine_mesh,
        in_specs=(P(ROW, COL, None), P(), P(), P(), P(), P(), P()),
        out_specs=(P(ROW, COL, None), P(ROW, COL, None)),
        check_vma=False,
    )
```

```python
import jax
import jax.numpy as jnp
from jax import lax
from jax.experimental import pallas as pl
from jax.experimental.pallas import tpu as pltpu
from jax.sharding import Mesh, PartitionSpec as P


AXES = ("zh", "y1", "y0", "core", "x1", "x0", "zl")
ROW = ("zh", "y1", "y0", "core")
COL = ("x1", "x0", "zl")
SPREAD = ("zh", "y1", "y0", "x1", "x0", "zl")
BF16 = jnp.bfloat16
F32 = jnp.float32
VMEM = pl.BlockSpec(memory_space=pltpu.VMEM)
SMEM = pl.BlockSpec(memory_space=pltpu.SMEM)


def kernel_call(body, outs, scratch=(), inputs=0, scalars=0, limit=24):
    call = pl.pallas_call(
        body,
        out_shape=[pltpu.VMEM(s, t) for s, t in outs],
        in_specs=[SMEM] * scalars + [VMEM] * inputs,
        out_specs=[VMEM] * len(outs),
        scratch_shapes=[pltpu.VMEM(s, t) for s, t in scratch],
        compiler_params=pltpu.CompilerParams(vmem_limit_bytes=limit << 20),
    )

    def run(*operands):
        near = [pltpu.with_memory_space_constraint(x, pltpu.VMEM) for x in operands[scalars:]]
        return call(*operands[:scalars], *near)

    return run


def chip(core, band, ring):
    turn = (band + 1) % 8
    y, side = divmod(turn, 2)
    z = (side + y) % 2
    if ring < 4:
        return ring, y, core + z
    return 7 - ring, (y + 1) % 4, (3 + core - z) % 4


def slot(core, band, ring):
    x, y, z = chip(core, band, ring)
    return (((z // 2) * 4 + y) * 4 + x) * 2 + z % 2


def device(core, band, ring):
    x, y, z = chip(core, band, ring)
    return ((((z // 2) * 4 + y) * 2 + core) * 4 + x) * 2 + z % 2


BLOCKS = [(core, band, ring) for core in range(2) for band in range(8) for ring in range(8)]


def block_route(row_step, column_step):
    route = []
    for core, band, ring in BLOCKS:
        row = (8 * core + band + row_step) % 16
        target = device(row // 8, row % 8, (ring + column_step) % 8)
        route.append((device(core, band, ring), target))
    return route


def notes():
    table = [None] * 128
    for core, band, ring in BLOCKS:
        slots = [slot(core, other // 8, other % 8) for other in range(64)]
        row = 8 * core + band
        table[device(core, band, ring)] = slots + [row == 0, row == 15, ring == 0, ring == 7]
    return jnp.array(table, jnp.int32)


def line_route(count, step):
    return [(i, i + step) for i in range(count) if 0 <= i + step < count]


def gather_body(notes, context, sent):
    channels = context.shape[-1]
    first = lax.broadcasted_iota(jnp.int32, (4, 8, channels), 1) < 4

    def step(row, carry):
        line = context[row].astype(F32)
        low = line[:32].reshape(4, 8, channels)
        high = line[32:].reshape(4, 8, channels)
        even = jnp.where(first, low, pltpu.roll(high, 4, 1))
        odd = jnp.where(first, pltpu.roll(low, 4, 1), high)
        for pair in range(4):
            place = 8 * (row // 2) + 2 * pair
            sent[notes[place], row % 2] = even[pair].astype(BF16)
            sent[notes[place + 1], row % 2] = odd[pair].astype(BF16)
        return carry

    lax.fori_loop(0, 16, step, 0)


def scatter_body(notes, landed, result):
    channels = result.shape[-1]
    first = lax.broadcasted_iota(jnp.int32, (8, channels), 0) < 4

    def step(row, carry):
        for pair in range(4):
            place = 8 * (row // 2) + 2 * pair
            even = landed[notes[place], row % 2].astype(F32)
            odd = landed[notes[place + 1], row % 2].astype(F32)
            low = jnp.where(first, even, pltpu.roll(odd, 4, 0))
            high = jnp.where(first, pltpu.roll(even, 4, 0), odd)
            result[row, 8 * pair : 8 * pair + 8] = low.astype(BF16)
            result[row, 32 + 8 * pair : 40 + 8 * pair] = high.astype(BF16)
        return carry

    lax.fori_loop(0, 16, step, 0)


def dilated_band(cells, kernel, hidden, shelves, spacing):
    channels = cells.shape[-1]
    reach = 4 * spacing
    place = lax.broadcasted_iota(jnp.int32, cells.shape, 1)
    left = jnp.where(place < reach, 0.0, pltpu.roll(cells, reach, 1))
    right = jnp.where(place >= 64 - reach, 0.0, pltpu.roll(cells, 64 - reach, 1))
    edge = jnp.zeros((spacing, 64, channels), BF16)
    for index, shelf in enumerate((left, cells, right)):
        shelves[index, :spacing] = edge
        shelves[index, spacing : spacing + 8] = shelf.astype(BF16)
        shelves[index, spacing + 8 : spacing + 8 + spacing] = edge
    stack = jnp.concatenate(
        [
            shelves[b, a * spacing : a * spacing + 8].reshape(512, channels)
            for a in range(3)
            for b in range(3)
        ],
        axis=1,
    )
    total = jnp.dot(stack, kernel[...], preferred_element_type=F32)
    hidden[...] = (total / (1.0 + jnp.exp(-total))).astype(BF16)


def first_dilated_body(landed, kernel, hidden0, hidden1, shelves):
    channels = landed.shape[-1]
    for i0, hidden in enumerate((hidden0, hidden1)):
        cells = landed[:, i0].astype(F32).reshape(8, 64, channels)
        dilated_band(cells, kernel, hidden, shelves, 1)


def settle(partial, sums, from_left, from_right, notes, i0, channels):
    place = lax.broadcasted_iota(jnp.int32, (128, channels), 0) % 16
    left = from_left[i0].astype(F32)
    right = from_right[i0].astype(F32)
    left = jnp.where(
        notes[66] == 1, jnp.where(place == 0, 0.0, pltpu.roll(left, 1, 0)), left
    )
    right = jnp.where(
        notes[67] == 1, jnp.where(place == 15, 0.0, pltpu.roll(right, 127, 0)), right
    )
    pieces = []
    for lane in range(0, channels, 128):
        inner = sums.at[i0, lane // 128]
        inner[...] = partial[i0, :, lane : lane + 128]
        inner[pl.ds(0, 128, stride=4)] = inner[pl.ds(0, 128, stride=4)] + left[:, lane : lane + 128]
        inner[pl.ds(3, 128, stride=4)] = inner[pl.ds(3, 128, stride=4)] + right[:, lane : lane + 128]
        pieces.append(inner[...].astype(BF16))
    return jnp.concatenate(pieces, 1)


def second_dilated_body(notes, partial, from_left, from_right, kernel, state, hidden0, hidden1, sums, shelves):
    channels = state.shape[-1]
    for i0, hidden in enumerate((hidden0, hidden1)):
        cells = settle(partial, sums, from_left, from_right, notes, i0, channels)
        state[:, i0] = cells.reshape(64, 8, channels)
        dilated_band(cells.astype(F32).reshape(8, 64, channels), kernel, hidden, shelves, 2)


def final_body(notes, partial, from_left, from_right, state, crop, sums):
    channels = state.shape[-1]
    for i0 in range(2):
        cells = settle(partial, sums, from_left, from_right, notes, i0, channels)
        state[:, i0] = cells.reshape(64, 8, channels)
    first = lax.broadcasted_iota(jnp.int32, (8, channels), 0) < 4
    for pair in range(4):
        place = 8 * (4 + pair // 2) + 4 + pair % 2
        top = state[place, 0].astype(F32)
        bottom = state[place, 1].astype(F32)
        crop[2 * pair] = jnp.where(first, top, pltpu.roll(bottom, 4, 0)).astype(BF16)
        crop[2 * pair + 1] = jnp.where(first, pltpu.roll(top, 4, 0), bottom).astype(BF16)


def edge_body(notes, up, down, hidden0, hidden1, kernel, to_left, to_right, above, below, wide):
    channels = up.shape[-1]
    blank = jnp.zeros((64, channels), BF16)
    above[:64] = blank
    above[64:] = up[...]
    below[:512] = down[...]
    below[512:] = blank
    start = pl.multiple_of(64 - 64 * notes[64], 64)
    lines = [above[pl.ds(start, 512)], hidden0[...], hidden1[...]]
    start = pl.multiple_of(64 * notes[65], 64)
    lines.append(below[pl.ds(start, 512)])
    for index, line in enumerate(lines):
        for lane in range(0, channels, 128):
            wide[index, lane // 128] = line[:, lane : lane + 128].astype(F32)
    for column, tap, sums in ((3, 0, to_right), (0, 2, to_left)):
        weights = kernel[:, tap].reshape(3 * channels, channels)
        lines = [
            jnp.concatenate(
                [
                    wide.at[line, lane][pl.ds(column, 128, stride=4)].astype(BF16)
                    for lane in range(channels // 128)
                ],
                1,
            )
            for line in range(4)
        ]
        stack = jnp.concatenate(
            [jnp.concatenate(lines[:3], 1), jnp.concatenate(lines[1:], 1)], 0
        )
        product = jnp.dot(stack, weights, preferred_element_type=F32).astype(BF16)
        sums[0] = product[:128]
        sums[1] = product[128:]


def plain_body(notes, up, down, hidden0, hidden1, state, kernel, partial, above, below):
    channels = up.shape[-1]
    blank = jnp.zeros((64, channels), BF16)
    above[:64] = blank
    above[64:] = up[...]
    below[:512] = down[...]
    below[512:] = blank
    over = above[pl.ds(pl.multiple_of(64 - 64 * notes[64], 64), 512)]
    under = below[pl.ds(pl.multiple_of(64 * notes[65], 64), 512)]
    lines = (over, hidden0[...], hidden1[...], under)
    place = lax.broadcasted_iota(jnp.int32, (512, channels), 0) % 4
    for i0 in range(2):
        stack = jnp.concatenate(lines[i0 : i0 + 3], 1)
        products = [
            jnp.dot(stack, kernel[:, tap].reshape(3 * channels, channels), preferred_element_type=F32)
            for tap in range(3)
        ]
        total = state[:, i0].reshape(512, channels).astype(F32) + products[1]
        total = total + jnp.where(place == 0, 0.0, pltpu.roll(products[0], 1, 0))
        total = total + jnp.where(place == 3, 0.0, pltpu.roll(products[2], 511, 0))
        partial[i0] = total


def crop_route(shift):
    route = []
    for row in range(16):
        for column in range(8):
            i5, i4, i32 = row // 8, row // 4 % 2, row % 4
            source = device(i4, 2 * i32 + i5, 4 * (column % 2) + column // 2)
            if 0 <= row + shift < 16:
                route.append((source, (row + shift) * 8 + column))
    return route


def crop_groups():
    return [
        [device(core, 2 * rows + i1, 4 * j4 + j32) for i1 in range(2) for j32 in range(4)]
        for core in range(2)
        for rows in range(4)
        for j4 in range(2)
    ]


def crop_cells(crop):
    channels = crop.shape[-1]
    crop = lax.all_to_all(
        crop, AXES, 0, 0, axis_index_groups=crop_groups(), tiled=True
    )
    crop = crop.reshape(2, 4, 2, 4, channels).transpose(0, 2, 1, 3, 4)
    return crop.reshape(4, 16, channels)


def fine_target(crop, lift_weight, fine_weight):
    width = fine_weight.shape[-1]
    low = lax.ppermute(crop[3:], AXES, crop_route(1))
    high = lax.ppermute(crop[:1], AXES, crop_route(-1))
    crop = lax.ppermute(crop, AXES, crop_route(0))
    crop = jnp.concatenate([low, crop, high], 0)
    low = lax.ppermute(crop[:, 15:], COL, line_route(8, 1))
    high = lax.ppermute(crop[:, :1], COL, line_route(8, -1))
    crop = jnp.concatenate([low, crop, high], 1)
    lifted = jnp.einsum("rcf,fg->rcg", crop, lift_weight, preferred_element_type=F32).astype(BF16)
    lifted = lifted.reshape(6, 18, 4, 4, width).transpose(0, 2, 1, 3, 4).reshape(24, 72, width)
    lifted = lifted[3:21, 3:69]
    target = lax.conv_general_dilated(
        lifted[None], fine_weight, (1, 1), ((0, 0), (0, 0)),
        dimension_numbers=("NHWC", "HWIO", "NHWC"), preferred_element_type=F32,
    )
    return target[0].astype(BF16)


def plain(hidden0, hidden1, state, kernel, own):
    channels = hidden0.shape[-1]
    up = lax.ppermute(hidden1, AXES, block_route(1, 0))
    down = lax.ppermute(hidden0, AXES, block_route(-1, 0))
    padded = [((576, channels), BF16)] * 2
    to_left, to_right = kernel_call(
        edge_body,
        [((2, 128, channels), BF16)] * 2,
        padded + [((4, 3, 512, 128), F32)],
        5, 1,
    )(own, up, down, hidden0, hidden1, kernel)
    from_left = lax.ppermute(to_right, AXES, block_route(0, 1))
    from_right = lax.ppermute(to_left, AXES, block_route(0, -1))
    (partial,) = kernel_call(plain_body, [((2, 512, channels), F32)], padded, 6, 1)(
        own, up, down, hidden0, hidden1, state, kernel
    )
    return partial, from_left, from_right


def shards(context, first_dilated_weight, first_plain_weight, second_dilated_weight,
           second_plain_weight, lift_weight, fine_weight):
    channels = context.shape[-1]
    own = notes()[lax.axis_index(AXES)]
    spread = (64, 2, 8, channels)
    band_shape = ((512, channels), BF16)
    (sent,) = kernel_call(gather_body, [(spread, BF16)], (), 1, 1)(own, context)
    state = lax.all_to_all(sent, SPREAD, 0, 0, tiled=True)
    hidden0, hidden1 = kernel_call(
        first_dilated_body, [band_shape] * 2, [((3, 10, 64, channels), BF16)], 2
    )(state, first_dilated_weight.reshape(9 * channels, channels))
    edges = plain(hidden0, hidden1, state, first_plain_weight, own)
    state, hidden0, hidden1 = kernel_call(
        second_dilated_body,
        [(spread, BF16), band_shape, band_shape],
        [((2, 3, 512, 128), F32), ((3, 12, 64, channels), BF16)],
        4, 1,
    )(own, *edges, second_dilated_weight.reshape(9 * channels, channels))
    edges = plain(hidden0, hidden1, state, second_plain_weight, own)
    state, crop = kernel_call(
        final_body, [(spread, BF16), ((8, 8, channels), BF16)], [((2, 3, 512, 128), F32)], 3, 1
    )(own, *edges)
    crop = crop_cells(crop)
    landed = lax.all_to_all(state, SPREAD, 0, 0, tiled=True)
    target = fine_target(crop, lift_weight, fine_weight)
    (result,) = kernel_call(scatter_body, [((16, 64, channels), BF16)], (), 1, 1)(own, landed)
    return result, target


def solution(mesh):
    fine_mesh = Mesh(mesh.devices.reshape((2,) * 7), AXES)
    return jax.shard_map(
        shards,
        mesh=fine_mesh,
        in_specs=(P(ROW, COL, None), P(), P(), P(), P(), P(), P()),
        out_specs=(P(ROW, COL, None), P(ROW, COL, None)),
        check_vma=False,
    )
```

```python
import jax
import jax.numpy as jnp
from jax import lax
from jax.experimental import pallas as pl
from jax.experimental.pallas import tpu as pltpu
from jax.sharding import Mesh, PartitionSpec as P


AXES = ("zh", "y1", "y0", "core", "x1", "x0", "zl")
ROW = ("zh", "y1", "y0", "core")
COL = ("x1", "x0", "zl")
SPREAD = ("zh", "y1", "y0", "x1", "x0", "zl")
BF16 = jnp.bfloat16
F32 = jnp.float32
VMEM = pl.BlockSpec(memory_space=pltpu.VMEM)
SMEM = pl.BlockSpec(memory_space=pltpu.SMEM)


def kernel_call(body, outs, scratch=(), inputs=0, scalars=0, limit=24):
    call = pl.pallas_call(
        body,
        out_shape=[pltpu.VMEM(s, t) for s, t in outs],
        in_specs=[SMEM] * scalars + [VMEM] * inputs,
        out_specs=[VMEM] * len(outs),
        scratch_shapes=[pltpu.VMEM(s, t) for s, t in scratch],
        compiler_params=pltpu.CompilerParams(vmem_limit_bytes=limit << 20),
    )

    def run(*operands):
        near = [pltpu.with_memory_space_constraint(x, pltpu.VMEM) for x in operands[scalars:]]
        return call(*operands[:scalars], *near)

    return run


def chip(core, band, ring):
    y, side = divmod((band + 1 - core) % 8, 2)
    z = core + (side + y) % 2
    if ring < 4:
        return ring, y, z
    if core == 0:
        return 7 - ring, (y - 1) % 4, 3 - z
    return 7 - ring, y, (z + 2) % 4


def slot(core, band, ring):
    x, y, z = chip(core, band, ring)
    return (((z // 2) * 4 + y) * 4 + x) * 2 + z % 2


def device(core, band, ring):
    x, y, z = chip(core, band, ring)
    return ((((z // 2) * 4 + y) * 2 + core) * 4 + x) * 2 + z % 2


BLOCKS = [(core, band, ring) for core in range(2) for band in range(8) for ring in range(8)]


def block_route(row_step, column_step):
    route = []
    for core, band, ring in BLOCKS:
        row = (8 * core + band + row_step) % 16
        target = device(row // 8, row % 8, (ring + column_step) % 8)
        route.append((device(core, band, ring), target))
    return route


def notes():
    table = [None] * 128
    for core, band, ring in BLOCKS:
        slots = [slot(core, other // 8, other % 8) for other in range(64)]
        row = 8 * core + band
        table[device(core, band, ring)] = slots + [row == 0, row == 15, ring == 0, ring == 7]
    return jnp.array(table, jnp.int32)


def line_route(count, step):
    return [(i, i + step) for i in range(count) if 0 <= i + step < count]


def gather_body(notes, context, sent):
    channels = context.shape[-1]
    first = lax.broadcasted_iota(jnp.int32, (4, 8, channels), 1) < 4

    def step(row, carry):
        line = context[row].astype(F32)
        low = line[:32].reshape(4, 8, channels)
        high = line[32:].reshape(4, 8, channels)
        even = jnp.where(first, low, pltpu.roll(high, 4, 1))
        odd = jnp.where(first, pltpu.roll(low, 4, 1), high)
        for pair in range(4):
            place = 8 * (row // 2) + 2 * pair
            sent[notes[place], row % 2] = even[pair].astype(BF16)
            sent[notes[place + 1], row % 2] = odd[pair].astype(BF16)
        return carry

    lax.fori_loop(0, 16, step, 0)


def scatter_body(notes, landed, result):
    channels = result.shape[-1]
    first = lax.broadcasted_iota(jnp.int32, (8, channels), 0) < 4

    def step(row, carry):
        for pair in range(4):
            place = 8 * (row // 2) + 2 * pair
            even = landed[notes[place], row % 2].astype(F32)
            odd = landed[notes[place + 1], row % 2].astype(F32)
            low = jnp.where(first, even, pltpu.roll(odd, 4, 0))
            high = jnp.where(first, pltpu.roll(even, 4, 0), odd)
            result[row, 8 * pair : 8 * pair + 8] = low.astype(BF16)
            result[row, 32 + 8 * pair : 40 + 8 * pair] = high.astype(BF16)
        return carry

    lax.fori_loop(0, 16, step, 0)


def dilated_band(cells, kernel, hidden, shelves, spacing):
    channels = cells.shape[-1]
    reach = 4 * spacing
    place = lax.broadcasted_iota(jnp.int32, cells.shape, 1)
    left = jnp.where(place < reach, 0.0, pltpu.roll(cells, reach, 1))
    right = jnp.where(place >= 64 - reach, 0.0, pltpu.roll(cells, 64 - reach, 1))
    edge = jnp.zeros((spacing, 64, channels), BF16)
    for index, shelf in enumerate((left, cells, right)):
        shelves[index, :spacing] = edge
        shelves[index, spacing : spacing + 8] = shelf.astype(BF16)
        shelves[index, spacing + 8 : spacing + 8 + spacing] = edge
    stack = jnp.concatenate(
        [
            shelves[b, a * spacing : a * spacing + 8].reshape(512, channels)
            for a in range(3)
            for b in range(3)
        ],
        axis=1,
    )
    total = jnp.dot(stack, kernel[...], preferred_element_type=F32)
    hidden[...] = (total / (1.0 + jnp.exp(-total))).astype(BF16)


def first_dilated_body(landed, kernel, hidden0, hidden1, shelves):
    channels = landed.shape[-1]
    for i0, hidden in enumerate((hidden0, hidden1)):
        cells = landed[:, i0].astype(F32).reshape(8, 64, channels)
        dilated_band(cells, kernel, hidden, shelves, 1)


def settle(partial, sums, from_left, from_right, notes, i0, channels):
    place = lax.broadcasted_iota(jnp.int32, (128, channels), 0) % 16
    left = from_left[i0].astype(F32)
    right = from_right[i0].astype(F32)
    left = jnp.where(
        notes[66] == 1, jnp.where(place == 0, 0.0, pltpu.roll(left, 1, 0)), left
    )
    right = jnp.where(
        notes[67] == 1, jnp.where(place == 15, 0.0, pltpu.roll(right, 127, 0)), right
    )
    pieces = []
    for lane in range(0, channels, 128):
        inner = sums.at[i0, lane // 128]
        inner[...] = partial[i0, :, lane : lane + 128]
        inner[pl.ds(0, 128, stride=4)] = inner[pl.ds(0, 128, stride=4)] + left[:, lane : lane + 128]
        inner[pl.ds(3, 128, stride=4)] = inner[pl.ds(3, 128, stride=4)] + right[:, lane : lane + 128]
        pieces.append(inner[...].astype(BF16))
    return jnp.concatenate(pieces, 1)


def second_dilated_body(notes, partial, from_left, from_right, kernel, state, hidden0, hidden1, sums, shelves):
    channels = state.shape[-1]
    for i0, hidden in enumerate((hidden0, hidden1)):
        cells = settle(partial, sums, from_left, from_right, notes, i0, channels)
        state[:, i0] = cells.reshape(64, 8, channels)
        dilated_band(cells.astype(F32).reshape(8, 64, channels), kernel, hidden, shelves, 2)


def final_body(notes, partial, from_left, from_right, state, crop, sums):
    channels = state.shape[-1]
    for i0 in range(2):
        cells = settle(partial, sums, from_left, from_right, notes, i0, channels)
        state[:, i0] = cells.reshape(64, 8, channels)
    first = lax.broadcasted_iota(jnp.int32, (8, channels), 0) < 4
    for pair in range(4):
        place = 8 * (4 + pair // 2) + 4 + pair % 2
        top = state[place, 0].astype(F32)
        bottom = state[place, 1].astype(F32)
        crop[2 * pair] = jnp.where(first, top, pltpu.roll(bottom, 4, 0)).astype(BF16)
        crop[2 * pair + 1] = jnp.where(first, pltpu.roll(top, 4, 0), bottom).astype(BF16)


def edge_body(notes, up, down, hidden0, hidden1, kernel, to_left, to_right, above, below, wide):
    channels = up.shape[-1]
    blank = jnp.zeros((64, channels), BF16)
    above[:64] = blank
    above[64:] = up[...]
    below[:512] = down[...]
    below[512:] = blank
    start = pl.multiple_of(64 - 64 * notes[64], 64)
    lines = [above[pl.ds(start, 512)], hidden0[...], hidden1[...]]
    start = pl.multiple_of(64 * notes[65], 64)
    lines.append(below[pl.ds(start, 512)])
    for index, line in enumerate(lines):
        for lane in range(0, channels, 128):
            wide[index, lane // 128] = line[:, lane : lane + 128].astype(F32)
    for column, tap, sums in ((3, 0, to_right), (0, 2, to_left)):
        weights = kernel[:, tap].reshape(3 * channels, channels)
        lines = [
            jnp.concatenate(
                [
                    wide.at[line, lane][pl.ds(column, 128, stride=4)].astype(BF16)
                    for lane in range(channels // 128)
                ],
                1,
            )
            for line in range(4)
        ]
        stack = jnp.concatenate(
            [jnp.concatenate(lines[:3], 1), jnp.concatenate(lines[1:], 1)], 0
        )
        product = jnp.dot(stack, weights, preferred_element_type=F32).astype(BF16)
        sums[0] = product[:128]
        sums[1] = product[128:]


def plain_body(notes, up, down, hidden0, hidden1, state, kernel, partial, above, below):
    channels = up.shape[-1]
    blank = jnp.zeros((64, channels), BF16)
    above[:64] = blank
    above[64:] = up[...]
    below[:512] = down[...]
    below[512:] = blank
    over = above[pl.ds(pl.multiple_of(64 - 64 * notes[64], 64), 512)]
    under = below[pl.ds(pl.multiple_of(64 * notes[65], 64), 512)]
    lines = (over, hidden0[...], hidden1[...], under)
    place = lax.broadcasted_iota(jnp.int32, (512, channels), 0) % 4
    for i0 in range(2):
        stack = jnp.concatenate(lines[i0 : i0 + 3], 1)
        products = [
            jnp.dot(stack, kernel[:, tap].reshape(3 * channels, channels), preferred_element_type=F32)
            for tap in range(3)
        ]
        total = state[:, i0].reshape(512, channels).astype(F32) + products[1]
        total = total + jnp.where(place == 0, 0.0, pltpu.roll(products[0], 1, 0))
        total = total + jnp.where(place == 3, 0.0, pltpu.roll(products[2], 511, 0))
        partial[i0] = total


def crop_route(shift):
    route = []
    for row in range(16):
        for column in range(8):
            i5, i4, i32 = row // 8, row // 4 % 2, row % 4
            source = device(i4, 2 * i32 + i5, 4 * (column % 2) + column // 2)
            if 0 <= row + shift < 16:
                route.append((source, (row + shift) * 8 + column))
    return route


def crop_groups():
    return [
        [device(core, 2 * rows + i1, 4 * j4 + j32) for i1 in range(2) for j32 in range(4)]
        for core in range(2)
        for rows in range(4)
        for j4 in range(2)
    ]


def crop_cells(crop):
    channels = crop.shape[-1]
    crop = lax.all_to_all(
        crop, AXES, 0, 0, axis_index_groups=crop_groups(), tiled=True
    )
    crop = crop.reshape(2, 4, 2, 4, channels).transpose(0, 2, 1, 3, 4)
    return crop.reshape(4, 16, channels)


def fine_target(crop, lift_weight, fine_weight):
    width = fine_weight.shape[-1]
    low = lax.ppermute(crop[3:], AXES, crop_route(1))
    high = lax.ppermute(crop[:1], AXES, crop_route(-1))
    crop = lax.ppermute(crop, AXES, crop_route(0))
    crop = jnp.concatenate([low, crop, high], 0)
    low = lax.ppermute(crop[:, 15:], COL, line_route(8, 1))
    high = lax.ppermute(crop[:, :1], COL, line_route(8, -1))
    crop = jnp.concatenate([low, crop, high], 1)
    lifted = jnp.einsum("rcf,fg->rcg", crop, lift_weight, preferred_element_type=F32).astype(BF16)
    lifted = lifted.reshape(6, 18, 4, 4, width).transpose(0, 2, 1, 3, 4).reshape(24, 72, width)
    lifted = lifted[3:21, 3:69]
    target = lax.conv_general_dilated(
        lifted[None], fine_weight, (1, 1), ((0, 0), (0, 0)),
        dimension_numbers=("NHWC", "HWIO", "NHWC"), preferred_element_type=F32,
    )
    return target[0].astype(BF16)


def plain(hidden0, hidden1, state, kernel, own):
    channels = hidden0.shape[-1]
    up = lax.ppermute(hidden1, AXES, block_route(1, 0))
    down = lax.ppermute(hidden0, AXES, block_route(-1, 0))
    padded = [((576, channels), BF16)] * 2
    to_left, to_right = kernel_call(
        edge_body,
        [((2, 128, channels), BF16)] * 2,
        padded + [((4, 3, 512, 128), F32)],
        5, 1,
    )(own, up, down, hidden0, hidden1, kernel)
    from_left = lax.ppermute(to_right, AXES, block_route(0, 1))
    from_right = lax.ppermute(to_left, AXES, block_route(0, -1))
    (partial,) = kernel_call(plain_body, [((2, 512, channels), F32)], padded, 6, 1)(
        own, up, down, hidden0, hidden1, state, kernel
    )
    return partial, from_left, from_right


def shards(context, first_dilated_weight, first_plain_weight, second_dilated_weight,
           second_plain_weight, lift_weight, fine_weight):
    channels = context.shape[-1]
    own = notes()[lax.axis_index(AXES)]
    spread = (64, 2, 8, channels)
    band_shape = ((512, channels), BF16)
    (sent,) = kernel_call(gather_body, [(spread, BF16)], (), 1, 1)(own, context)
    state = lax.all_to_all(sent, SPREAD, 0, 0, tiled=True)
    hidden0, hidden1 = kernel_call(
        first_dilated_body, [band_shape] * 2, [((3, 10, 64, channels), BF16)], 2
    )(state, first_dilated_weight.reshape(9 * channels, channels))
    edges = plain(hidden0, hidden1, state, first_plain_weight, own)
    state, hidden0, hidden1 = kernel_call(
        second_dilated_body,
        [(spread, BF16), band_shape, band_shape],
        [((2, 3, 512, 128), F32), ((3, 12, 64, channels), BF16)],
        4, 1,
    )(own, *edges, second_dilated_weight.reshape(9 * channels, channels))
    edges = plain(hidden0, hidden1, state, second_plain_weight, own)
    state, crop = kernel_call(
        final_body, [(spread, BF16), ((8, 8, channels), BF16)], [((2, 3, 512, 128), F32)], 3, 1
    )(own, *edges)
    crop = crop_cells(crop)
    landed = lax.all_to_all(state, SPREAD, 0, 0, tiled=True)
    target = fine_target(crop, lift_weight, fine_weight)
    (result,) = kernel_call(scatter_body, [((16, 64, channels), BF16)], (), 1, 1)(own, landed)
    return result, target


def solution(mesh):
    fine_mesh = Mesh(mesh.devices.reshape((2,) * 7), AXES)
    return jax.shard_map(
        shards,
        mesh=fine_mesh,
        in_specs=(P(ROW, COL, None), P(), P(), P(), P(), P(), P()),
        out_specs=(P(ROW, COL, None), P(ROW, COL, None)),
        check_vma=False,
    )
```

```python
import jax
import jax.numpy as jnp
from jax import lax
from jax.experimental import pallas as pl
from jax.experimental.pallas import tpu as pltpu
from jax.sharding import Mesh, PartitionSpec as P


AXES = ("zh", "y1", "y0", "core", "x1", "x0", "zl")
ROW = ("zh", "y1", "y0", "core")
COL = ("x1", "x0", "zl")
SPREAD = ("zh", "y1", "y0", "x1", "x0", "zl")
BF16 = jnp.bfloat16
F32 = jnp.float32
VMEM = pl.BlockSpec(memory_space=pltpu.VMEM)
SMEM = pl.BlockSpec(memory_space=pltpu.SMEM)


def kernel_call(body, outs, scratch=(), inputs=0, scalars=0, limit=24):
    call = pl.pallas_call(
        body,
        out_shape=[pltpu.VMEM(s, t) for s, t in outs],
        in_specs=[SMEM] * scalars + [VMEM] * inputs,
        out_specs=[VMEM] * len(outs),
        scratch_shapes=[pltpu.VMEM(s, t) for s, t in scratch],
        compiler_params=pltpu.CompilerParams(vmem_limit_bytes=limit << 20),
    )

    def run(*operands):
        near = [pltpu.with_memory_space_constraint(x, pltpu.VMEM) for x in operands[scalars:]]
        return call(*operands[:scalars], *near)

    return run


def chip(core, band, ring):
    y, side = divmod((band + 1 - core) % 8, 2)
    z = core + (side + y) % 2
    if ring < 4:
        return ring, y, z
    if core == 0:
        return 7 - ring, (y - 1) % 4, 3 - z
    return 7 - ring, y, (z + 2) % 4


def slot(core, band, ring):
    x, y, z = chip(core, band, ring)
    return (((z // 2) * 4 + y) * 4 + x) * 2 + z % 2


def device(core, band, ring):
    x, y, z = chip(core, band, ring)
    return ((((z // 2) * 4 + y) * 2 + core) * 4 + x) * 2 + z % 2


BLOCKS = [(core, band, ring) for core in range(2) for band in range(8) for ring in range(8)]


def block_route(row_step, column_step):
    route = []
    for core, band, ring in BLOCKS:
        row = (8 * core + band + row_step) % 16
        target = device(row // 8, row % 8, (ring + column_step) % 8)
        route.append((device(core, band, ring), target))
    return route


def meets(start, length, low, high):
    return start <= high and start + length > low


def crop_picks(core, band, ring):
    first_row = 16 * core + 2 * band
    rows = [
        4 * int(meets(first_row + 32, 2, 8 * m - 1, 8 * m + 8)) for m in range(8)
    ]
    columns = [
        sum(g for g in range(4) if meets(4 * ring + 32 * g, 4, 16 * c - 1, 16 * c + 16))
        for c in range(8)
    ]
    return rows + columns


def window_rows(row, core):
    bands = []
    for line in range(4 * row - 1, 4 * row + 5):
        owner, band = divmod(line % 32 // 2, 8)
        bands.append(band if 0 <= line < 64 and owner == core else -1)
    return bands


def window_rings(column):
    starts = range(16 * column - 4, 16 * column + 20, 4)
    return [start % 32 // 4 if 0 <= start < 128 else -1 for start in starts]


FIRST_ROW, LAST_ROW, FIRST_RING, LAST_RING = range(64, 68)
PICK_ROW, PICK_COLUMN, OWN_ROWS, OTHER_ROWS, RINGS = 68, 76, 84, 90, 96


def notes():
    table = [None] * 128
    for core, band, ring in BLOCKS:
        slots = [slot(core, other // 8, other % 8) for other in range(64)]
        line = 8 * core + band
        place = device(core, band, ring)
        row, column = divmod(place, 8)
        table[place] = (
            slots
            + [line == 0, line == 15, ring == 0, ring == 7]
            + crop_picks(core, band, ring)
            + window_rows(row, core)
            + window_rows(row ^ 1, core)
            + window_rings(column)
        )
    return jnp.array(table, jnp.int32)


def gather_body(notes, context, sent):
    channels = context.shape[-1]
    first = lax.broadcasted_iota(jnp.int32, (4, 8, channels), 1) < 4

    def step(row, carry):
        line = context[row].astype(F32)
        low = line[:32].reshape(4, 8, channels)
        high = line[32:].reshape(4, 8, channels)
        even = jnp.where(first, low, pltpu.roll(high, 4, 1))
        odd = jnp.where(first, pltpu.roll(low, 4, 1), high)
        for pair in range(4):
            place = 8 * (row // 2) + 2 * pair
            sent[notes[place], row % 2] = even[pair].astype(BF16)
            sent[notes[place + 1], row % 2] = odd[pair].astype(BF16)
        return carry

    lax.fori_loop(0, 16, step, 0)


def scatter_body(notes, landed, result):
    channels = result.shape[-1]
    first = lax.broadcasted_iota(jnp.int32, (8, channels), 0) < 4

    def step(row, carry):
        for pair in range(4):
            place = 8 * (row // 2) + 2 * pair
            even = landed[notes[place], row % 2].astype(F32)
            odd = landed[notes[place + 1], row % 2].astype(F32)
            low = jnp.where(first, even, pltpu.roll(odd, 4, 0))
            high = jnp.where(first, pltpu.roll(even, 4, 0), odd)
            result[row, 8 * pair : 8 * pair + 8] = low.astype(BF16)
            result[row, 32 + 8 * pair : 40 + 8 * pair] = high.astype(BF16)
        return carry

    lax.fori_loop(0, 16, step, 0)


def dilated_band(cells, kernel, hidden, shelves, spacing):
    channels = cells.shape[-1]
    reach = 4 * spacing
    place = lax.broadcasted_iota(jnp.int32, cells.shape, 1)
    left = jnp.where(place < reach, 0.0, pltpu.roll(cells, reach, 1))
    right = jnp.where(place >= 64 - reach, 0.0, pltpu.roll(cells, 64 - reach, 1))
    edge = jnp.zeros((spacing, 64, channels), BF16)
    for index, shelf in enumerate((left, cells, right)):
        shelves[index, :spacing] = edge
        shelves[index, spacing : spacing + 8] = shelf.astype(BF16)
        shelves[index, spacing + 8 : spacing + 8 + spacing] = edge
    stack = jnp.concatenate(
        [
            shelves[b, a * spacing : a * spacing + 8].reshape(512, channels)
            for a in range(3)
            for b in range(3)
        ],
        axis=1,
    )
    total = jnp.dot(stack, kernel[...], preferred_element_type=F32)
    hidden[...] = (total / (1.0 + jnp.exp(-total))).astype(BF16)


def first_dilated_body(landed, kernel, hidden0, hidden1, shelves):
    channels = landed.shape[-1]
    for i0, hidden in enumerate((hidden0, hidden1)):
        cells = landed[:, i0].astype(F32).reshape(8, 64, channels)
        dilated_band(cells, kernel, hidden, shelves, 1)


def settle(partial, sums, from_left, from_right, notes, i0, channels):
    place = lax.broadcasted_iota(jnp.int32, (128, channels), 0) % 16
    left = from_left[i0].astype(F32)
    right = from_right[i0].astype(F32)
    left = jnp.where(
        notes[FIRST_RING] == 1, jnp.where(place == 0, 0.0, pltpu.roll(left, 1, 0)), left
    )
    right = jnp.where(
        notes[LAST_RING] == 1, jnp.where(place == 15, 0.0, pltpu.roll(right, 127, 0)), right
    )
    pieces = []
    for lane in range(0, channels, 128):
        inner = sums.at[i0, lane // 128]
        inner[...] = partial[i0, :, lane : lane + 128]
        inner[pl.ds(0, 128, stride=4)] = inner[pl.ds(0, 128, stride=4)] + left[:, lane : lane + 128]
        inner[pl.ds(3, 128, stride=4)] = inner[pl.ds(3, 128, stride=4)] + right[:, lane : lane + 128]
        pieces.append(inner[...].astype(BF16))
    return jnp.concatenate(pieces, 1)


def second_dilated_body(notes, partial, from_left, from_right, kernel, state, hidden0, hidden1, sums, shelves):
    channels = state.shape[-1]
    for i0, hidden in enumerate((hidden0, hidden1)):
        cells = settle(partial, sums, from_left, from_right, notes, i0, channels)
        state[:, i0] = cells.reshape(64, 8, channels)
        dilated_band(cells.astype(F32).reshape(8, 64, channels), kernel, hidden, shelves, 2)


def final_body(notes, partial, from_left, from_right, outgoing, sums, crop):
    channels = outgoing.shape[-1]
    for i0 in range(2):
        cells = settle(partial, sums, from_left, from_right, notes, i0, channels)
        outgoing[:, i0] = cells.reshape(64, 8, channels)
    first = lax.broadcasted_iota(jnp.int32, (8, channels), 0) < 4
    for pair in range(4):
        place = 8 * (4 + pair // 2) + 4 + pair % 2
        top = outgoing[place, 0].astype(F32)
        bottom = outgoing[place, 1].astype(F32)
        crop[2 * pair] = jnp.where(first, top, pltpu.roll(bottom, 4, 0)).astype(BF16)
        crop[2 * pair + 1] = jnp.where(first, pltpu.roll(top, 4, 0), bottom).astype(BF16)

    def step(chip_row, carry):
        for column in range(8):
            pick = notes[PICK_ROW + chip_row] + notes[PICK_COLUMN + column]
            outgoing[8 * chip_row + column, 2] = crop[pick]
        return carry

    lax.fori_loop(0, 8, step, 0)


def window_body(notes, landed, own, other):
    channels = own.shape[-1]
    first = lax.broadcasted_iota(jnp.int32, (8, channels), 0) < 4
    for window, rows in ((own, OWN_ROWS), (other, OTHER_ROWS)):
        for line in range(6):
            band = notes[rows + line]
            for tile in range(3):
                halves = []
                for side in range(2):
                    ring = notes[RINGS + 2 * tile + side]
                    there = jnp.logical_and(band >= 0, ring >= 0)
                    place = notes[jnp.where(there, 8 * band + ring, 0)]
                    block = landed[place, 2].astype(F32)
                    halves.append(jnp.where(there, block, 0.0))
                even, odd = halves
                if line % 2:
                    joined = jnp.where(first, even, pltpu.roll(odd, 4, 0))
                else:
                    joined = jnp.where(first, pltpu.roll(even, 4, 0), odd)
                window[line, 8 * tile : 8 * tile + 8] = joined.astype(BF16)


def edge_body(notes, up, down, hidden0, hidden1, kernel, to_left, to_right, above, below, wide):
    channels = up.shape[-1]
    blank = jnp.zeros((64, channels), BF16)
    above[:64] = blank
    above[64:] = up[...]
    below[:512] = down[...]
    below[512:] = blank
    start = pl.multiple_of(64 - 64 * notes[FIRST_ROW], 64)
    lines = [above[pl.ds(start, 512)], hidden0[...], hidden1[...]]
    start = pl.multiple_of(64 * notes[LAST_ROW], 64)
    lines.append(below[pl.ds(start, 512)])
    for index, line in enumerate(lines):
        for lane in range(0, channels, 128):
            wide[index, lane // 128] = line[:, lane : lane + 128].astype(F32)
    for column, tap, sums in ((3, 0, to_right), (0, 2, to_left)):
        weights = kernel[:, tap].reshape(3 * channels, channels)
        lines = [
            jnp.concatenate(
                [
                    wide.at[line, lane][pl.ds(column, 128, stride=4)].astype(BF16)
                    for lane in range(channels // 128)
                ],
                1,
            )
            for line in range(4)
        ]
        stack = jnp.concatenate(
            [jnp.concatenate(lines[:3], 1), jnp.concatenate(lines[1:], 1)], 0
        )
        product = jnp.dot(stack, weights, preferred_element_type=F32).astype(BF16)
        sums[0] = product[:128]
        sums[1] = product[128:]


def plain_body(notes, up, down, hidden0, hidden1, state, kernel, partial, above, below):
    channels = up.shape[-1]
    blank = jnp.zeros((64, channels), BF16)
    above[:64] = blank
    above[64:] = up[...]
    below[:512] = down[...]
    below[512:] = blank
    over = above[pl.ds(pl.multiple_of(64 - 64 * notes[FIRST_ROW], 64), 512)]
    under = below[pl.ds(pl.multiple_of(64 * notes[LAST_ROW], 64), 512)]
    lines = (over, hidden0[...], hidden1[...], under)
    place = lax.broadcasted_iota(jnp.int32, (512, channels), 0) % 4
    for i0 in range(2):
        stack = jnp.concatenate(lines[i0 : i0 + 3], 1)
        products = [
            jnp.dot(stack, kernel[:, tap].reshape(3 * channels, channels), preferred_element_type=F32)
            for tap in range(3)
        ]
        total = state[:, i0].reshape(512, channels).astype(F32) + products[1]
        total = total + jnp.where(place == 0, 0.0, pltpu.roll(products[0], 1, 0))
        total = total + jnp.where(place == 3, 0.0, pltpu.roll(products[2], 511, 0))
        partial[i0] = total


def fine_target(crop, lift_weight, fine_weight):
    width = fine_weight.shape[-1]
    lifted = jnp.einsum("rcf,fg->rcg", crop, lift_weight, preferred_element_type=F32).astype(BF16)
    lifted = lifted.reshape(6, 24, 4, 4, width).transpose(0, 2, 1, 3, 4).reshape(24, 96, width)
    lifted = lifted[3:21, 15:81]
    target = lax.conv_general_dilated(
        lifted[None], fine_weight, (1, 1), ((0, 0), (0, 0)),
        dimension_numbers=("NHWC", "HWIO", "NHWC"), preferred_element_type=F32,
    )
    return target[0].astype(BF16)


def plain(hidden0, hidden1, state, kernel, own):
    channels = hidden0.shape[-1]
    up = lax.ppermute(hidden1, AXES, block_route(1, 0))
    down = lax.ppermute(hidden0, AXES, block_route(-1, 0))
    padded = [((576, channels), BF16)] * 2
    to_left, to_right = kernel_call(
        edge_body,
        [((2, 128, channels), BF16)] * 2,
        padded + [((4, 3, 512, 128), F32)],
        5, 1,
    )(own, up, down, hidden0, hidden1, kernel)
    from_left = lax.ppermute(to_right, AXES, block_route(0, 1))
    from_right = lax.ppermute(to_left, AXES, block_route(0, -1))
    (partial,) = kernel_call(plain_body, [((2, 512, channels), F32)], padded, 6, 1)(
        own, up, down, hidden0, hidden1, state, kernel
    )
    return partial, from_left, from_right


def shards(context, first_dilated_weight, first_plain_weight, second_dilated_weight,
           second_plain_weight, lift_weight, fine_weight):
    channels = context.shape[-1]
    own = notes()[lax.axis_index(AXES)]
    spread = (64, 2, 8, channels)
    band_shape = ((512, channels), BF16)
    (sent,) = kernel_call(gather_body, [(spread, BF16)], (), 1, 1)(own, context)
    state = lax.all_to_all(sent, SPREAD, 0, 0, tiled=True)
    hidden0, hidden1 = kernel_call(
        first_dilated_body, [band_shape] * 2, [((3, 10, 64, channels), BF16)], 2
    )(state, first_dilated_weight.reshape(9 * channels, channels))
    edges = plain(hidden0, hidden1, state, first_plain_weight, own)
    state, hidden0, hidden1 = kernel_call(
        second_dilated_body,
        [(spread, BF16), band_shape, band_shape],
        [((2, 3, 512, 128), F32), ((3, 12, 64, channels), BF16)],
        4, 1,
    )(own, *edges, second_dilated_weight.reshape(9 * channels, channels))
    edges = plain(hidden0, hidden1, state, second_plain_weight, own)
    (outgoing,) = kernel_call(
        final_body,
        [((64, 3, 8, channels), BF16)],
        [((2, 3, 512, 128), F32), ((8, 8, channels), BF16)],
        3, 1,
    )(own, *edges)
    landed = lax.all_to_all(outgoing, SPREAD, 0, 0, tiled=True)
    window, other = kernel_call(window_body, [((6, 24, channels), BF16)] * 2, (), 1, 1)(
        own, landed
    )
    swapped = lax.ppermute(other, "core", [(0, 1), (1, 0)])
    (result,) = kernel_call(scatter_body, [((16, 64, channels), BF16)], (), 1, 1)(own, landed)
    target = fine_target(window + swapped, lift_weight, fine_weight)
    return result, target


def solution(mesh):
    fine_mesh = Mesh(mesh.devices.reshape((2,) * 7), AXES)
    return jax.shard_map(
        shards,
        mesh=fine_mesh,
        in_specs=(P(ROW, COL, None), P(), P(), P(), P(), P(), P()),
        out_specs=(P(ROW, COL, None), P(ROW, COL, None)),
        check_vma=False,
    )
```

```python
import jax
import jax.numpy as jnp
from jax import lax
from jax.experimental import pallas as pl
from jax.experimental.pallas import tpu as pltpu
from jax.sharding import Mesh, PartitionSpec as P


AXES = ("zh", "y1", "y0", "core", "x1", "x0", "zl")
ROW = ("zh", "y1", "y0", "core")
COL = ("x1", "x0", "zl")
SPREAD = ("zh", "y1", "y0", "x1", "x0", "zl")
BF16 = jnp.bfloat16
F32 = jnp.float32
VMEM = pl.BlockSpec(memory_space=pltpu.VMEM)
SMEM = pl.BlockSpec(memory_space=pltpu.SMEM)


def kernel_call(body, outs, scratch=(), inputs=0, scalars=0, limit=24):
    call = pl.pallas_call(
        body,
        out_shape=[pltpu.VMEM(s, t) for s, t in outs],
        in_specs=[SMEM] * scalars + [VMEM] * inputs,
        out_specs=[VMEM] * len(outs),
        scratch_shapes=[pltpu.VMEM(s, t) for s, t in scratch],
        compiler_params=pltpu.CompilerParams(vmem_limit_bytes=limit << 20),
    )

    def run(*operands):
        near = [pltpu.with_memory_space_constraint(x, pltpu.VMEM) for x in operands[scalars:]]
        return call(*operands[:scalars], *near)

    return run


def chip(core, band, ring):
    y, side = divmod((band + 1 - core) % 8, 2)
    z = core + (side + y) % 2
    if ring < 4:
        return ring, y, z
    if core == 0:
        return 7 - ring, (y - 1) % 4, 3 - z
    return 7 - ring, y, (z + 2) % 4


def slot(core, band, ring):
    x, y, z = chip(core, band, ring)
    return (((z // 2) * 4 + y) * 4 + x) * 2 + z % 2


def device(core, band, ring):
    x, y, z = chip(core, band, ring)
    return ((((z // 2) * 4 + y) * 2 + core) * 4 + x) * 2 + z % 2


BLOCKS = [(core, band, ring) for core in range(2) for band in range(8) for ring in range(8)]


def block_route(row_step, column_step):
    route = []
    for core, band, ring in BLOCKS:
        row = (8 * core + band + row_step) % 16
        target = device(row // 8, row % 8, (ring + column_step) % 8)
        route.append((device(core, band, ring), target))
    return route


def meets(start, length, low, high):
    return start <= high and start + length > low


def crop_picks(core, band, ring):
    first_row = 16 * core + 2 * band
    rows = [
        4 * int(meets(first_row + 32, 2, 8 * m - 1, 8 * m + 8)) for m in range(8)
    ]
    columns = [
        sum(g for g in range(4) if meets(4 * ring + 32 * g, 4, 16 * c - 1, 16 * c + 16))
        for c in range(8)
    ]
    return rows + columns


def window_rows(row, core):
    bands = []
    for line in range(4 * row - 1, 4 * row + 5):
        owner, band = divmod(line % 32 // 2, 8)
        bands.append(band if 0 <= line < 64 and owner == core else -1)
    return bands


def window_rings(column):
    starts = range(16 * column - 4, 16 * column + 20, 4)
    return [start % 32 // 4 if 0 <= start < 128 else -1 for start in starts]


FIRST_ROW, LAST_ROW, FIRST_RING, LAST_RING = range(64, 68)
PICK_ROW, PICK_COLUMN, OWN_ROWS, OTHER_ROWS, RINGS = 68, 76, 84, 90, 96


def notes():
    table = [None] * 128
    for core, band, ring in BLOCKS:
        slots = [slot(core, other // 8, other % 8) for other in range(64)]
        line = 8 * core + band
        place = device(core, band, ring)
        row, column = divmod(place, 8)
        table[place] = (
            slots
            + [line == 0, line == 15, ring == 0, ring == 7]
            + crop_picks(core, band, ring)
            + window_rows(row, core)
            + window_rows(row ^ 1, core)
            + window_rings(column)
        )
    return jnp.array(table, jnp.int32)


def gather_body(notes, context, sent):
    channels = context.shape[-1]
    first = lax.broadcasted_iota(jnp.int32, (4, 8, channels), 1) < 4

    def step(row, carry):
        line = context[row].astype(F32)
        low = line[:32].reshape(4, 8, channels)
        high = line[32:].reshape(4, 8, channels)
        even = jnp.where(first, low, pltpu.roll(high, 4, 1))
        odd = jnp.where(first, pltpu.roll(low, 4, 1), high)
        for pair in range(4):
            place = 8 * (row // 2) + 2 * pair
            sent[notes[place], row % 2] = even[pair].astype(BF16)
            sent[notes[place + 1], row % 2] = odd[pair].astype(BF16)
        return carry

    lax.fori_loop(0, 16, step, 0)


def scatter_body(notes, landed, result, near, departures):
    channels = result.shape[-1]
    first = lax.broadcasted_iota(jnp.int32, (8, channels), 0) < 4

    def send(part):
        rows = pl.ds(4 * part, 4)
        return pltpu.make_async_copy(near.at[rows], result.at[rows], departures.at[part])

    def step(row, carry):
        for pair in range(4):
            place = 8 * (row // 2) + 2 * pair
            even = landed[notes[place], row % 2].astype(F32)
            odd = landed[notes[place + 1], row % 2].astype(F32)
            low = jnp.where(first, even, pltpu.roll(odd, 4, 0))
            high = jnp.where(first, pltpu.roll(even, 4, 0), odd)
            near[row, 8 * pair : 8 * pair + 8] = low.astype(BF16)
            near[row, 32 + 8 * pair : 40 + 8 * pair] = high.astype(BF16)
        return carry

    for part in range(4):
        lax.fori_loop(4 * part, 4 * part + 4, step, 0)
        send(part).start()
    for part in range(4):
        send(part).wait()


def scatter(notes, landed):
    shape = (16, 64, landed.shape[-1])
    return pl.pallas_call(
        scatter_body,
        out_shape=jax.ShapeDtypeStruct(shape, BF16),
        in_specs=[SMEM, VMEM],
        out_specs=pl.BlockSpec(memory_space=pltpu.HBM),
        scratch_shapes=[pltpu.VMEM(shape, BF16), pltpu.SemaphoreType.DMA((4,))],
        compiler_params=pltpu.CompilerParams(vmem_limit_bytes=24 << 20),
    )(notes, pltpu.with_memory_space_constraint(landed, pltpu.VMEM))


def dilated_band(cells, kernel, hidden, shelves, spacing):
    channels = cells.shape[-1]
    reach = 4 * spacing
    place = lax.broadcasted_iota(jnp.int32, cells.shape, 1)
    left = jnp.where(place < reach, 0.0, pltpu.roll(cells, reach, 1))
    right = jnp.where(place >= 64 - reach, 0.0, pltpu.roll(cells, 64 - reach, 1))
    edge = jnp.zeros((spacing, 64, channels), BF16)
    for index, shelf in enumerate((left, cells, right)):
        shelves[index, :spacing] = edge
        shelves[index, spacing : spacing + 8] = shelf.astype(BF16)
        shelves[index, spacing + 8 : spacing + 8 + spacing] = edge
    stack = jnp.concatenate(
        [
            shelves[b, a * spacing : a * spacing + 8].reshape(512, channels)
            for a in range(3)
            for b in range(3)
        ],
        axis=1,
    )
    total = jnp.dot(stack, kernel[...], preferred_element_type=F32)
    hidden[...] = (total / (1.0 + jnp.exp(-total))).astype(BF16)


def first_dilated_body(landed, kernel, hidden0, hidden1, shelves):
    channels = landed.shape[-1]
    for i0, hidden in enumerate((hidden0, hidden1)):
        cells = landed[:, i0].astype(F32).reshape(8, 64, channels)
        dilated_band(cells, kernel, hidden, shelves, 1)


def settle(partial, sums, from_left, from_right, notes, i0, channels):
    place = lax.broadcasted_iota(jnp.int32, (128, channels), 0) % 16
    left = from_left[i0].astype(F32)
    right = from_right[i0].astype(F32)
    left = jnp.where(
        notes[FIRST_RING] == 1, jnp.where(place == 0, 0.0, pltpu.roll(left, 1, 0)), left
    )
    right = jnp.where(
        notes[LAST_RING] == 1, jnp.where(place == 15, 0.0, pltpu.roll(right, 127, 0)), right
    )
    pieces = []
    for lane in range(0, channels, 128):
        inner = sums.at[i0, lane // 128]
        inner[...] = partial[i0, :, lane : lane + 128]
        inner[pl.ds(0, 128, stride=4)] = inner[pl.ds(0, 128, stride=4)] + left[:, lane : lane + 128]
        inner[pl.ds(3, 128, stride=4)] = inner[pl.ds(3, 128, stride=4)] + right[:, lane : lane + 128]
        pieces.append(inner[...].astype(BF16))
    return jnp.concatenate(pieces, 1)


def second_dilated_body(notes, partial, from_left, from_right, kernel, state, hidden0, hidden1, sums, shelves):
    channels = state.shape[-1]
    for i0, hidden in enumerate((hidden0, hidden1)):
        cells = settle(partial, sums, from_left, from_right, notes, i0, channels)
        state[:, i0] = cells.reshape(64, 8, channels)
        dilated_band(cells.astype(F32).reshape(8, 64, channels), kernel, hidden, shelves, 2)


def final_body(notes, partial, from_left, from_right, outgoing, sums, crop):
    channels = outgoing.shape[-1]
    for i0 in range(2):
        cells = settle(partial, sums, from_left, from_right, notes, i0, channels)
        outgoing[:, i0] = cells.reshape(64, 8, channels)
    first = lax.broadcasted_iota(jnp.int32, (8, channels), 0) < 4
    for pair in range(4):
        place = 8 * (4 + pair // 2) + 4 + pair % 2
        top = outgoing[place, 0].astype(F32)
        bottom = outgoing[place, 1].astype(F32)
        crop[2 * pair] = jnp.where(first, top, pltpu.roll(bottom, 4, 0)).astype(BF16)
        crop[2 * pair + 1] = jnp.where(first, pltpu.roll(top, 4, 0), bottom).astype(BF16)

    def step(chip_row, carry):
        for column in range(8):
            pick = notes[PICK_ROW + chip_row] + notes[PICK_COLUMN + column]
            outgoing[8 * chip_row + column, 2] = crop[pick]
        return carry

    lax.fori_loop(0, 8, step, 0)


def window_body(notes, landed, own, other):
    channels = own.shape[-1]
    first = lax.broadcasted_iota(jnp.int32, (8, channels), 0) < 4
    for window, rows in ((own, OWN_ROWS), (other, OTHER_ROWS)):
        for line in range(6):
            band = notes[rows + line]
            for tile in range(3):
                halves = []
                for side in range(2):
                    ring = notes[RINGS + 2 * tile + side]
                    there = jnp.logical_and(band >= 0, ring >= 0)
                    place = notes[jnp.where(there, 8 * band + ring, 0)]
                    block = landed[place, 2].astype(F32)
                    halves.append(jnp.where(there, block, 0.0))
                even, odd = halves
                if line % 2:
                    joined = jnp.where(first, even, pltpu.roll(odd, 4, 0))
                else:
                    joined = jnp.where(first, pltpu.roll(even, 4, 0), odd)
                window[line, 8 * tile : 8 * tile + 8] = joined.astype(BF16)


def shifted_products(products, place):
    left, centre, right = products
    total = centre + jnp.where(place == 0, 0.0, pltpu.roll(left, 1, 0))
    return total + jnp.where(place == 3, 0.0, pltpu.roll(right, 511, 0))


def own_body(hidden0, hidden1, state, kernel, partial, own_left, own_right, wide):
    channels = hidden0.shape[-1]
    place = lax.broadcasted_iota(jnp.int32, (512, channels), 0) % 4
    lines = jnp.concatenate([hidden0[...], hidden1[...]], 1)
    for i0 in range(2):
        products = [
            jnp.dot(
                lines,
                kernel[1 - i0 : 3 - i0, tap].reshape(2 * channels, channels),
                preferred_element_type=F32,
            )
            for tap in range(3)
        ]
        for product, start, sums in ((products[0], 3, own_right), (products[2], 0, own_left)):
            for lane in range(0, channels, 128):
                wide[...] = product[:, lane : lane + 128]
                sums[i0, :, lane : lane + 128] = wide[pl.ds(start, 128, stride=4)]
        total = shifted_products(products, place)
        partial[i0] = state[:, i0].reshape(512, channels).astype(F32) + total


def edge_body(notes, up, down, own_left, own_right, kernel, to_left, to_right, wide):
    channels = up.shape[-1]
    place = lax.broadcasted_iota(jnp.int32, (128, channels), 0)
    for i0, line, wrap, far, turn in (
        (0, up, notes[FIRST_ROW], place < 16, 16),
        (1, down, notes[LAST_ROW], place >= 112, 112),
    ):
        for lane in range(0, channels, 128):
            wide[lane // 128] = line[:, lane : lane + 128].astype(F32)
        for start, tap, own, sums in ((3, 0, own_right, to_right), (0, 2, own_left, to_left)):
            cells = jnp.concatenate(
                [wide.at[lane][pl.ds(start, 128, stride=4)] for lane in range(channels // 128)], 1
            )
            moved = jnp.where(far, 0.0, pltpu.roll(cells, turn, 0))
            cells = jnp.where(wrap == 1, moved, cells).astype(BF16)
            product = jnp.dot(cells, kernel[2 * i0, tap], preferred_element_type=F32)
            sums[i0] = (own[i0] + product).astype(BF16)


def rest_body(notes, up, down, partial, kernel, total, above, below):
    channels = up.shape[-1]
    blank = jnp.zeros((64, channels), BF16)
    above[:64] = blank
    above[64:] = up[...]
    below[:512] = down[...]
    below[512:] = blank
    over = above[pl.ds(pl.multiple_of(64 - 64 * notes[FIRST_ROW], 64), 512)]
    under = below[pl.ds(pl.multiple_of(64 * notes[LAST_ROW], 64), 512)]
    place = lax.broadcasted_iota(jnp.int32, (512, channels), 0) % 4
    for i0, line in enumerate((over, under)):
        products = [
            jnp.dot(line, kernel[2 * i0, tap], preferred_element_type=F32) for tap in range(3)
        ]
        total[i0] = partial[i0] + shifted_products(products, place)


def fine_body(own, swapped, lift, fine, target, image, taps, merged):
    channels, width = own.shape[-1], fine.shape[-1]
    window = own[...].astype(F32) + swapped[...].astype(F32)
    window = window.astype(BF16).reshape(144, channels)
    lifted = jnp.dot(window, lift[...], preferred_element_type=F32)
    lifted = lifted.astype(BF16).astype(F32).reshape(6, 24, 16 * width)
    image[...] = jnp.zeros(image.shape, BF16)
    taps[...] = jnp.zeros(taps.shape, BF16)
    for a in range(3):
        for b in range(3):
            row = 128 * (3 * a + b)
            taps[row : row + width, :width] = fine[a, b]
    for phase, v, shift in ((0, 3, 3), (1, 0, 4), (2, 1, 4), (3, 2, 4), (4, 3, 4), (5, 0, 5)):
        for u in range(4):
            lane = width * (4 * u + v)
            block = pltpu.roll(lifted[:, :, lane : lane + width], 24 - shift, 1)
            block = block[:, :16].astype(BF16)
            for line in range(6):
                row = 4 * (line - 1) + u + 1
                if 0 <= row < 18:
                    image[row, phase, :, :width] = block[line]
    for v in range(4):
        stack = jnp.concatenate(
            [
                image[a : a + 16, v + b].reshape(256, 128)
                for a in range(3)
                for b in range(3)
            ],
            1,
        )
        merged[pl.ds(v, 256, stride=4)] = jnp.dot(
            stack, taps[...], preferred_element_type=F32
        )
    target[...] = merged[...].astype(BF16)[:, :width].reshape(target.shape)


def fine_target(own, swapped, lift_weight, fine_weight):
    width = fine_weight.shape[-1]
    near = [
        pltpu.with_memory_space_constraint(x, pltpu.VMEM)
        for x in (own, swapped, lift_weight, fine_weight)
    ]
    return pl.pallas_call(
        fine_body,
        out_shape=jax.ShapeDtypeStruct((16, 64, width), BF16),
        in_specs=[VMEM] * 4,
        scratch_shapes=[
            pltpu.VMEM((18, 6, 16, 128), BF16),
            pltpu.VMEM((9 * 128, 128), BF16),
            pltpu.VMEM((1024, 128), F32),
        ],
        compiler_params=pltpu.CompilerParams(vmem_limit_bytes=24 << 20),
    )(*near)


def plain(hidden0, hidden1, state, kernel, own):
    channels = hidden0.shape[-1]
    up = lax.ppermute(hidden1, AXES, block_route(1, 0))
    down = lax.ppermute(hidden0, AXES, block_route(-1, 0))
    edge = (2, 128, channels)
    body = (2, 512, channels)
    partial, own_left, own_right = kernel_call(
        own_body, [(body, F32), (edge, F32), (edge, F32)], [((512, 128), F32)], 4
    )(hidden0, hidden1, state, kernel)
    to_left, to_right = kernel_call(
        edge_body, [(edge, BF16)] * 2, [((3, 512, 128), F32)], 5, 1
    )(own, up, down, own_left, own_right, kernel)
    from_left = lax.ppermute(to_right, AXES, block_route(0, 1))
    from_right = lax.ppermute(to_left, AXES, block_route(0, -1))
    (total,) = kernel_call(rest_body, [(body, F32)], [((576, channels), BF16)] * 2, 4, 1)(
        own, up, down, partial, kernel
    )
    return total, from_left, from_right


def shards(context, first_dilated_weight, first_plain_weight, second_dilated_weight,
           second_plain_weight, lift_weight, fine_weight):
    channels = context.shape[-1]
    own = notes()[lax.axis_index(AXES)]
    spread = (64, 2, 8, channels)
    band_shape = ((512, channels), BF16)
    (sent,) = kernel_call(gather_body, [(spread, BF16)], (), 1, 1)(own, context)
    state = lax.all_to_all(sent, SPREAD, 0, 0, tiled=True)
    hidden0, hidden1 = kernel_call(
        first_dilated_body, [band_shape] * 2, [((3, 10, 64, channels), BF16)], 2
    )(state, first_dilated_weight.reshape(9 * channels, channels))
    edges = plain(hidden0, hidden1, state, first_plain_weight, own)
    state, hidden0, hidden1 = kernel_call(
        second_dilated_body,
        [(spread, BF16), band_shape, band_shape],
        [((2, 3, 512, 128), F32), ((3, 12, 64, channels), BF16)],
        4, 1,
    )(own, *edges, second_dilated_weight.reshape(9 * channels, channels))
    edges = plain(hidden0, hidden1, state, second_plain_weight, own)
    (outgoing,) = kernel_call(
        final_body,
        [((64, 3, 8, channels), BF16)],
        [((2, 3, 512, 128), F32), ((8, 8, channels), BF16)],
        3, 1,
    )(own, *edges)
    landed = lax.all_to_all(outgoing, SPREAD, 0, 0, tiled=True)
    window, other = kernel_call(window_body, [((6, 24, channels), BF16)] * 2, (), 1, 1)(
        own, landed
    )
    swapped = lax.ppermute(other, "core", [(0, 1), (1, 0)])
    result = scatter(own, landed)
    target = fine_target(window, swapped, lift_weight, fine_weight)
    return result, target


def solution(mesh):
    fine_mesh = Mesh(mesh.devices.reshape((2,) * 7), AXES)
    return jax.shard_map(
        shards,
        mesh=fine_mesh,
        in_specs=(P(ROW, COL, None), P(), P(), P(), P(), P(), P()),
        out_specs=(P(ROW, COL, None), P(ROW, COL, None)),
        check_vma=False,
    )
```

```python
import jax
import jax.numpy as jnp
import numpy as np
from jax import lax
from jax.experimental import pallas as pl
from jax.experimental.pallas import tpu as pltpu
from jax.sharding import Mesh, PartitionSpec as P


AXES = ("zh", "y1", "y0", "core", "x1", "x0", "zl")
ROW = ("zh", "y1", "y0", "core")
COL = ("x1", "x0", "zl")
SPREAD = ("zh", "y1", "y0", "x1", "x0", "zl")
BF16 = jnp.bfloat16
F32 = jnp.float32
VMEM = pl.BlockSpec(memory_space=pltpu.VMEM)
SMEM = pl.BlockSpec(memory_space=pltpu.SMEM)


def kernel_call(body, outs, scratch=(), inputs=0, scalars=0, limit=24):
    def whole(*refs):
        return body(*[ref.at[0] for ref in refs[:scalars]], *refs[scalars:])

    call = pl.pallas_call(
        whole,
        out_shape=[pltpu.VMEM(s, t) for s, t in outs],
        in_specs=[SMEM] * scalars + [VMEM] * inputs,
        out_specs=[VMEM] * len(outs),
        scratch_shapes=[pltpu.VMEM(s, t) for s, t in scratch],
        compiler_params=pltpu.CompilerParams(vmem_limit_bytes=limit << 20),
    )

    def run(*operands):
        near = [pltpu.with_memory_space_constraint(x, pltpu.VMEM) for x in operands[scalars:]]
        return call(*operands[:scalars], *near)

    return run


def ladder(core, band, ring):
    turn = (band + 1 - core) % 8
    y = turn // 2
    z = core + (turn + y) % 2
    if ring < 4:
        return ring, y, z
    return 7 - ring, (y + 3 * (1 - core)) % 4, (3 - z) * (1 - core) + (z + 2) % 4 * core


def chip(core, band, ring):
    x, y, z = ladder(core, band, ring)
    return x, (5 - y) % 4, z


def slot(core, band, ring):
    x, y, z = chip(core, band, ring)
    return (((z // 2) * 4 + y) * 4 + x) * 2 + z % 2


def device(core, band, ring):
    x, y, z = chip(core, band, ring)
    return ((((z // 2) * 4 + y) * 2 + core) * 4 + x) * 2 + z % 2


BLOCKS = [(core, band, ring) for core in range(2) for band in range(8) for ring in range(8)]


def block_route(row_step, column_step):
    route = []
    for core, band, ring in BLOCKS:
        row = (8 * core + band + row_step) % 16
        target = device(row // 8, row % 8, (ring + column_step) % 8)
        route.append((device(core, band, ring), target))
    return route


def meets(start, length, low, high):
    return start <= high and start + length > low


def crop_picks(core, band, ring):
    first_row = 16 * core + 2 * band
    rows = [
        4 * int(meets(first_row + 32, 2, 8 * m - 1, 8 * m + 8)) for m in range(8)
    ]
    columns = [
        sum(g for g in range(4) if meets(4 * ring + 32 * g, 4, 16 * c - 1, 16 * c + 16))
        for c in range(8)
    ]
    return rows + columns


def window_rows(row, core):
    bands = []
    for line in range(4 * row - 1, 4 * row + 5):
        owner, band = divmod(line % 32 // 2, 8)
        bands.append(band if 0 <= line < 64 and owner == core else -1)
    return bands


def window_rings(column):
    starts = range(16 * column - 4, 16 * column + 20, 4)
    return [start % 32 // 4 if 0 <= start < 128 else -1 for start in starts]


FIRST_ROW, LAST_ROW, FIRST_RING, LAST_RING = range(64, 68)
PICK_ROW, PICK_COLUMN, OWN_ROWS, OTHER_ROWS, RINGS = 68, 76, 84, 90, 96


def notes():
    table = [None] * 128
    for core, band, ring in BLOCKS:
        slots = [slot(core, other // 8, other % 8) for other in range(64)]
        line = 8 * core + band
        place = device(core, band, ring)
        row, column = divmod(place, 8)
        table[place] = (
            slots
            + [line == 0, line == 15, ring == 0, ring == 7]
            + crop_picks(core, band, ring)
            + window_rows(row, core)
            + window_rows(row ^ 1, core)
            + window_rings(column)
        )
    return np.array(table, np.int32)


def gather_body(place, context, sent):
    own_core = place[0] // 8 % 2
    channels = context.shape[-1]
    first = lax.broadcasted_iota(jnp.int32, (4, 8, channels), 1) < 4

    def step(row, carry):
        line = context[row].astype(F32)
        low = line[:32].reshape(4, 8, channels)
        high = line[32:].reshape(4, 8, channels)
        even = jnp.where(first, low, pltpu.roll(high, 4, 1))
        odd = jnp.where(first, pltpu.roll(low, 4, 1), high)
        for pair in range(4):
            sent[slot(own_core, row // 2, 2 * pair), row % 2] = even[pair].astype(BF16)
            sent[slot(own_core, row // 2, 2 * pair + 1), row % 2] = odd[pair].astype(BF16)
        return carry

    lax.fori_loop(0, 16, step, 0)


def pick_body(place, table, own):
    own[...] = table[0]


def own_notes(place):
    table = notes()
    table = np.pad(table, ((0, 0), (0, 128 - table.shape[1]))).reshape(128, 1, 128)
    return pl.pallas_call(
        pick_body,
        grid_spec=pltpu.PrefetchScalarGridSpec(
            num_scalar_prefetch=1,
            grid=(1,),
            in_specs=[pl.BlockSpec((1, 1, 128), lambda step, place: (place[0], 0, 0))],
            out_specs=pl.BlockSpec((1, 128), lambda step, place: (0, 0)),
        ),
        out_shape=jax.ShapeDtypeStruct((1, 128), jnp.int32),
        compiler_params=pltpu.CompilerParams(vmem_limit_bytes=1 << 20),
    )(place.reshape(1), jnp.asarray(table))


def scatter_body(notes, landed, result, near, departures):
    notes = notes.at[0]
    channels = result.shape[-1]
    first = lax.broadcasted_iota(jnp.int32, (8, channels), 0) < 4

    def send(part):
        rows = pl.ds(4 * part, 4)
        return pltpu.make_async_copy(near.at[rows], result.at[rows], departures.at[part])

    def step(row, carry):
        for pair in range(4):
            place = 8 * (row // 2) + 2 * pair
            even = landed[notes[place], row % 2].astype(F32)
            odd = landed[notes[place + 1], row % 2].astype(F32)
            low = jnp.where(first, even, pltpu.roll(odd, 4, 0))
            high = jnp.where(first, pltpu.roll(even, 4, 0), odd)
            near[row, 8 * pair : 8 * pair + 8] = low.astype(BF16)
            near[row, 32 + 8 * pair : 40 + 8 * pair] = high.astype(BF16)
        return carry

    for part in range(4):
        lax.fori_loop(4 * part, 4 * part + 4, step, 0)
        send(part).start()
    for part in range(4):
        send(part).wait()


def scatter(notes, landed):
    shape = (16, 64, landed.shape[-1])
    return pl.pallas_call(
        scatter_body,
        out_shape=jax.ShapeDtypeStruct(shape, BF16),
        in_specs=[SMEM, VMEM],
        out_specs=pl.BlockSpec(memory_space=pltpu.HBM),
        scratch_shapes=[pltpu.VMEM(shape, BF16), pltpu.SemaphoreType.DMA((4,))],
        compiler_params=pltpu.CompilerParams(vmem_limit_bytes=24 << 20),
    )(notes, pltpu.with_memory_space_constraint(landed, pltpu.VMEM))


def dilated_blocks(cells, kernel, shelves, spacing):
    channels = cells[0].shape[-1]
    count = len(cells)
    grid = jnp.stack(cells).reshape(count * 8, 16, channels)
    place = lax.broadcasted_iota(jnp.int32, grid.shape, 1)
    left = jnp.where(place < spacing, 0.0, pltpu.roll(grid, spacing, 1))
    right = jnp.where(place >= 16 - spacing, 0.0, pltpu.roll(grid, 16 - spacing, 1))
    edge = jnp.zeros((count, spacing, 16, channels), BF16)
    for index, shelf in enumerate((left, grid, right)):
        shelves[index, :, :spacing] = edge
        shelves[index, :, spacing : spacing + 8] = shelf.astype(BF16).reshape(
            count, 8, 16, channels
        )
        shelves[index, :, spacing + 8 : spacing + 8 + spacing] = edge
    stack = jnp.concatenate(
        [
            shelves[b, :, a * spacing : a * spacing + 8].reshape(128 * count, channels)
            for a in range(3)
            for b in range(3)
        ],
        axis=1,
    )
    total = jnp.dot(stack, kernel[...], preferred_element_type=F32)
    total = total / (1.0 + jnp.exp(-total))
    return total.astype(BF16).reshape(count, 128, channels)


def first_dilated_body(landed, kernel, state, hidden0, hidden1, shelves, wide):
    channels = landed.shape[-1]
    for i0, hidden in enumerate((hidden0, hidden1)):
        pieces = [[] for _ in range(4)]
        for lane in range(0, channels, 128):
            part = wide.at[lane // 128]
            part[...] = landed[:, i0, :, lane : lane + 128].astype(F32).reshape(512, 128)
            for column in range(4):
                pieces[column].append(part[pl.ds(column, 128, stride=4)])
        cells = [jnp.concatenate(piece, 1) for piece in pieces]
        for column in range(4):
            state[i0, column] = cells[column].astype(BF16)
        hidden[...] = dilated_blocks(cells, kernel, shelves, 1)


def settle(total, from_left, from_right, notes, i0):
    place = lax.broadcasted_iota(jnp.int32, from_left.shape[1:], 0) % 16
    left = from_left[i0].astype(F32)
    right = from_right[i0].astype(F32)
    moved = jnp.where(place == 0, 0.0, pltpu.roll(left, 1, 0))
    left = jnp.where(notes[FIRST_RING] == 1, moved, left)
    moved = jnp.where(place == 15, 0.0, pltpu.roll(right, 127, 0))
    right = jnp.where(notes[LAST_RING] == 1, moved, right)
    first = total[i0, 0] + left
    last = total[i0, 3] + right
    return first.astype(BF16), last.astype(BF16)


def inner_dilated_body(total, kernel, state, hidden, shelves):
    cells = []
    for i0 in range(2):
        for column in range(2):
            rounded = total[i0, column + 1].astype(BF16)
            state[i0, column] = rounded
            cells.append(rounded.astype(F32))
    hidden[...] = dilated_blocks(cells, kernel, shelves, 2)


def outer_dilated_body(
    notes, total, from_left, from_right, kernel, inner_state, inner_hidden,
    state, hidden0, hidden1, shelves,
):
    cells = []
    for i0 in range(2):
        first, last = settle(total, from_left, from_right, notes, i0)
        state[i0, 0] = first
        state[i0, 1:3] = inner_state[i0]
        state[i0, 3] = last
        cells += [first.astype(F32), last.astype(F32)]
    outer = dilated_blocks(cells, kernel, shelves, 2)
    for i0, hidden in enumerate((hidden0, hidden1)):
        hidden[0] = outer[2 * i0]
        hidden[1:3] = inner_hidden[2 * i0 : 2 * i0 + 2]
        hidden[3] = outer[2 * i0 + 1]


def final_body(notes, total, from_left, from_right, outgoing, wide, crop):
    channels = outgoing.shape[-1]
    for i0 in range(2):
        first, last = settle(total, from_left, from_right, notes, i0)
        cells = (first.astype(F32), total[i0, 1], total[i0, 2], last.astype(F32))
        for lane in range(0, channels, 128):
            part = wide.at[lane // 128]
            for column in range(4):
                part[pl.ds(column, 128, stride=4)] = cells[column][:, lane : lane + 128]
            block = part[...].astype(BF16).reshape(64, 8, 128)
            outgoing[:, i0, :, lane : lane + 128] = block
    first = lax.broadcasted_iota(jnp.int32, (8, channels), 0) < 4
    for pair in range(4):
        place = 8 * (4 + pair // 2) + 4 + pair % 2
        top = outgoing[place, 0].astype(F32)
        bottom = outgoing[place, 1].astype(F32)
        crop[2 * pair] = jnp.where(first, top, pltpu.roll(bottom, 4, 0)).astype(BF16)
        crop[2 * pair + 1] = jnp.where(first, pltpu.roll(top, 4, 0), bottom).astype(BF16)

    def step(chip_row, carry):
        for column in range(8):
            pick = notes[PICK_ROW + chip_row] + notes[PICK_COLUMN + column]
            outgoing[8 * chip_row + column, 2] = crop[pick]
        return carry

    lax.fori_loop(0, 8, step, 0)


def window_body(notes, landed, own, other):
    channels = own.shape[-1]
    first = lax.broadcasted_iota(jnp.int32, (8, channels), 0) < 4
    for window, rows in ((own, OWN_ROWS), (other, OTHER_ROWS)):
        for line in range(6):
            band = notes[rows + line]
            for tile in range(3):
                halves = []
                for side in range(2):
                    ring = notes[RINGS + 2 * tile + side]
                    there = jnp.logical_and(band >= 0, ring >= 0)
                    place = notes[jnp.where(there, 8 * band + ring, 0)]
                    block = landed[place, 2].astype(F32)
                    halves.append(jnp.where(there, block, 0.0))
                even, odd = halves
                if line % 2:
                    joined = jnp.where(first, even, pltpu.roll(odd, 4, 0))
                else:
                    joined = jnp.where(first, pltpu.roll(even, 4, 0), odd)
                window[line, 8 * tile : 8 * tile + 8] = joined.astype(BF16)


def shifted_products(products):
    left, centre, right = products
    blocks = []
    for column in range(4):
        block = centre[column]
        if column > 0:
            block = block + left[column - 1]
        if column < 3:
            block = block + right[column + 1]
        blocks.append(block)
    return blocks


def own_body(hidden0, hidden1, state, kernel, partial, own_left, own_right):
    channels = hidden0.shape[-1]
    lines = jnp.concatenate(
        [hidden0[...].reshape(512, channels), hidden1[...].reshape(512, channels)], 1
    )
    for i0 in range(2):
        products = [
            jnp.dot(
                lines,
                kernel[1 - i0 : 3 - i0, tap].reshape(2 * channels, channels),
                preferred_element_type=F32,
            ).reshape(4, 128, channels)
            for tap in range(3)
        ]
        own_right[i0] = products[0][3]
        own_left[i0] = products[2][0]
        for column, block in enumerate(shifted_products(products)):
            partial[i0, column] = state[i0, column].astype(F32) + block


def edge_body(notes, up, down, own_left, own_right, kernel, to_left, to_right):
    channels = up.shape[-1]
    place = lax.broadcasted_iota(jnp.int32, (128, channels), 0)
    for i0, line, wrap, far, turn in (
        (0, up, notes[FIRST_ROW], place < 16, 16),
        (1, down, notes[LAST_ROW], place >= 112, 112),
    ):
        for column, tap, own, sums in ((3, 0, own_right, to_right), (0, 2, own_left, to_left)):
            cells = line[column].astype(F32)
            moved = jnp.where(far, 0.0, pltpu.roll(cells, turn, 0))
            cells = jnp.where(wrap == 1, moved, cells).astype(BF16)
            product = jnp.dot(cells, kernel[2 * i0, tap], preferred_element_type=F32)
            sums[i0] = (own[i0] + product).astype(BF16)


def rest_body(notes, up, down, partial, kernel, total, above, below):
    channels = up.shape[-1]
    blank = jnp.zeros((4, 16, channels), BF16)
    above[:, :16] = blank
    above[:, 16:] = up[...]
    below[:, :128] = down[...]
    below[:, 128:] = blank
    over = above[:, pl.ds(pl.multiple_of(16 - 16 * notes[FIRST_ROW], 16), 128)]
    under = below[:, pl.ds(pl.multiple_of(16 * notes[LAST_ROW], 16), 128)]
    for i0, line in enumerate((over, under)):
        line = line.reshape(512, channels)
        products = [
            jnp.dot(line, kernel[2 * i0, tap], preferred_element_type=F32).reshape(
                4, 128, channels
            )
            for tap in range(3)
        ]
        for column, block in enumerate(shifted_products(products)):
            total[i0, column] = partial[i0, column] + block


def fine_body(own, swapped, lift, fine, target, image, taps, merged):
    channels, width = own.shape[-1], fine.shape[-1]
    window = own[...].astype(F32) + swapped[...].astype(F32)
    window = window.astype(BF16).reshape(144, channels)
    lifted = jnp.dot(window, lift[...], preferred_element_type=F32)
    lifted = lifted.astype(BF16).astype(F32).reshape(6, 24, 16 * width)
    image[...] = jnp.zeros(image.shape, BF16)
    taps[...] = jnp.zeros(taps.shape, BF16)
    for a in range(3):
        for b in range(3):
            row = 128 * (3 * a + b)
            taps[row : row + width, :width] = fine[a, b]
    for phase, v, shift in ((0, 3, 3), (1, 0, 4), (2, 1, 4), (3, 2, 4), (4, 3, 4), (5, 0, 5)):
        for u in range(4):
            lane = width * (4 * u + v)
            block = pltpu.roll(lifted[:, :, lane : lane + width], 24 - shift, 1)
            block = block[:, :16].astype(BF16)
            for line in range(6):
                row = 4 * (line - 1) + u + 1
                if 0 <= row < 18:
                    image[row, phase, :, :width] = block[line]
    for v in range(4):
        stack = jnp.concatenate(
            [
                image[a : a + 16, v + b].reshape(256, 128)
                for a in range(3)
                for b in range(3)
            ],
            1,
        )
        merged[pl.ds(v, 256, stride=4)] = jnp.dot(
            stack, taps[...], preferred_element_type=F32
        )
    target[...] = merged[...].astype(BF16)[:, :width].reshape(target.shape)


def fine_target(own, swapped, lift_weight, fine_weight):
    width = fine_weight.shape[-1]
    near = [
        pltpu.with_memory_space_constraint(x, pltpu.VMEM)
        for x in (own, swapped, lift_weight, fine_weight)
    ]
    return pl.pallas_call(
        fine_body,
        out_shape=jax.ShapeDtypeStruct((16, 64, width), BF16),
        in_specs=[VMEM] * 4,
        scratch_shapes=[
            pltpu.VMEM((18, 6, 16, 128), BF16),
            pltpu.VMEM((9 * 128, 128), BF16),
            pltpu.VMEM((1024, 128), F32),
        ],
        compiler_params=pltpu.CompilerParams(vmem_limit_bytes=24 << 20),
    )(*near)


def plain(hidden0, hidden1, state, kernel, own):
    channels = hidden0.shape[-1]
    up = lax.ppermute(hidden1, AXES, block_route(1, 0))
    down = lax.ppermute(hidden0, AXES, block_route(-1, 0))
    edge = (2, 128, channels)
    body = (2, 4, 128, channels)
    partial, own_left, own_right = kernel_call(
        own_body, [(body, F32), (edge, F32), (edge, F32)], (), 4
    )(hidden0, hidden1, state, kernel)
    to_left, to_right = kernel_call(
        edge_body, [(edge, BF16)] * 2, (), 5, 1
    )(own, up, down, own_left, own_right, kernel)
    from_left = lax.ppermute(to_right, AXES, block_route(0, 1))
    from_right = lax.ppermute(to_left, AXES, block_route(0, -1))
    (total,) = kernel_call(rest_body, [(body, F32)], [((4, 144, channels), BF16)] * 2, 4, 1)(
        own, up, down, partial, kernel
    )
    return total, from_left, from_right


def shards(context, first_dilated_weight, first_plain_weight, second_dilated_weight,
           second_plain_weight, lift_weight, fine_weight):
    channels = context.shape[-1]
    place = lax.axis_index(AXES)
    own = own_notes(place)
    spread = (64, 2, 8, channels)
    line = ((4, 128, channels), BF16)
    body = ((2, 4, 128, channels), BF16)
    inner = ((2, 2, 128, channels), BF16)
    columns = ((3, 512, 128), F32)
    shelves = ((3, 4, 12, 16, channels), BF16)
    (sent,) = kernel_call(gather_body, [(spread, BF16)], (), 1, 1)(
        place.reshape(1, 1), context
    )
    landed = lax.all_to_all(sent, SPREAD, 0, 0, tiled=True)
    state, hidden0, hidden1 = kernel_call(
        first_dilated_body,
        [body, line, line],
        [((3, 4, 10, 16, channels), BF16), columns],
        2,
    )(landed, first_dilated_weight.reshape(9 * channels, channels))
    total, from_left, from_right = plain(hidden0, hidden1, state, first_plain_weight, own)
    weights = second_dilated_weight.reshape(9 * channels, channels)
    inner_state, inner_hidden = kernel_call(
        inner_dilated_body, [inner, ((4, 128, channels), BF16)], [shelves], 2
    )(total, weights)
    state, hidden0, hidden1 = kernel_call(
        outer_dilated_body, [body, line, line], [shelves], 6, 1
    )(own, total, from_left, from_right, weights, inner_state, inner_hidden)
    edges = plain(hidden0, hidden1, state, second_plain_weight, own)
    (outgoing,) = kernel_call(
        final_body,
        [((64, 3, 8, channels), BF16)],
        [columns, ((8, 8, channels), BF16)],
        3, 1,
    )(own, *edges)
    landed = lax.all_to_all(outgoing, SPREAD, 0, 0, tiled=True)
    window, other = kernel_call(window_body, [((6, 24, channels), BF16)] * 2, (), 1, 1)(
        own, landed
    )
    swapped = lax.ppermute(other, "core", [(0, 1), (1, 0)])
    result = scatter(own, landed)
    target = fine_target(window, swapped, lift_weight, fine_weight)
    return result, target


def solution(mesh):
    fine_mesh = Mesh(mesh.devices.reshape((2,) * 7), AXES)
    return jax.shard_map(
        shards,
        mesh=fine_mesh,
        in_specs=(P(ROW, COL, None), P(), P(), P(), P(), P(), P()),
        out_specs=(P(ROW, COL, None), P(ROW, COL, None)),
        check_vma=False,
    )
```
